128 devices in a mesh: dp: 4 (over z_lo, core), ctx: 32 (over z_hi, x, y).
Axes of the slice: x: 4, y: 4, z: 4 (z_hi: 2, z_lo: 2; z = z_hi * 2 + z_lo), core: 2. Of those that a mesh axis runs over, the one named last changes fastest.
Arguments:
- queries: bfloat16 [4, 4096, 4096], P('dp', 'ctx'), may hold values from -256 to 256
- keys: bfloat16 [4, 4096, 4096], P('dp', 'ctx'), may hold values from -4 to 4
- gate: bfloat16 [4, 4096, 4096], P('dp', 'ctx'), may hold values from -6 to 6
- values: bfloat16 [4, 4096, 4096], P('dp', 'ctx'), may hold values from -6 to 6
- grad_out: bfloat16 [4, 4096, 4096], P('dp', 'ctx'), may hold values from -3 to 3
- doc_start: int32 [4, 4096], P('dp', 'ctx'), may hold values from 0 to 4095, as said below
- filter_taps: float32 [128, 4096], replicated, may hold values from -0.5 to 0.5
Outputs:
- grad_queries: bfloat16 [4, 4096, 4096], P('dp', 'ctx')
- grad_keys: bfloat16 [4, 4096, 4096], P('dp', 'ctx')
- grad_gate: bfloat16 [4, 4096, 4096], P('dp', 'ctx')
- grad_values: bfloat16 [4, 4096, 4096], P('dp', 'ctx')
- grad_filter: float32 [128, 4096], replicated
The draws below stay inside these ranges and needn't reach their ends.
Inputs may be any that keep to these rules, and one draw needn't show every extreme that they name: `doc_start`: entry t of a sequence is the first position of the document that holds position t: it never exceeds t and never falls along the sequence; every document has at most 640 positions, and every sequence holds one of exactly 640 positions.
All inputs are finite; a program needn't handle non-finite values.
Results may differ from the reference program's by a relative error of at most 0.0087.
Values may be sent and summed in bfloat16 or wider, within the bound.
No kernel may reach another device: no remote copies, remote signals or barrier semaphores. Data moves between devices by JAX's collectives and lax.ppermute only.
A program may use at most 192 MiB of HBM per device.

```python
import jax
import jax.numpy as jnp
from jax import lax

HEADS = 32
HEAD_DIM = 128
FILT = 128
TOK_DEV = 128
ATT_HOPS = 5
CHANNELS = 4096
SEQ = 4096
BATCH = 4


def query_key_pair(key):
    shape = (BATCH, SEQ, HEADS, HEAD_DIM)
    first_key = jax.random.fold_in(key, 101)
    second_key = jax.random.fold_in(key, 102)
    query_out = jnp.clip(jax.random.normal(first_key, shape, jnp.float32), -4.0, 4.0)
    key_out = jnp.clip(jax.random.normal(second_key, shape, jnp.float32), -4.0, 4.0)
    query_out = jnp.clip(query_out, -256.0, 256.0).reshape(BATCH, SEQ, CHANNELS)
    key_out = jnp.clip(key_out, -4.0, 4.0).reshape(BATCH, SEQ, CHANNELS)
    return (query_out.astype(jnp.bfloat16), key_out.astype(jnp.bfloat16))


def draw_queries(key, part):
    return query_key_pair(key)[0]


def draw_keys(key, part):
    return query_key_pair(key)[1]


def draw_doc_start(key, part):
    doc_count = SEQ // TOK_DEV + 2
    most_len = ATT_HOPS * TOK_DEV
    rest = jax.random.randint(jax.random.fold_in(key, 31), (BATCH, doc_count - 2), TOK_DEV, most_len + 1)
    first = jax.random.randint(jax.random.fold_in(key, 32), (BATCH, 1), 1, TOK_DEV)
    longest = jnp.full((BATCH, 1), most_len, jnp.int32)
    lengths = jnp.concatenate((first.astype(jnp.int32), longest, rest.astype(jnp.int32)), 1)
    starts = (jnp.cumsum(lengths, 1) - lengths).astype(jnp.int32)
    positions = jnp.arange(SEQ, dtype=jnp.int32)
    passed = starts[:, None, :] <= positions[None, :, None]
    return jnp.max(jnp.where(passed, starts[:, None, :], 0), -1).astype(jnp.int32)


def block_levels(key, extent, shards, smallest, high):
    factor_of, own = 1.0, jax.random.fold_in(key, 6)
    for axis_at, parts in shards:
        steps = jnp.exp(jax.random.uniform(jax.random.fold_in(own, axis_at), (parts,), jnp.float32, smallest / len(shards), high / len(shards)))
        factor_of = factor_of * jnp.repeat(steps, extent[axis_at] // parts).reshape([-1 if axis == axis_at else 1 for axis in range(len(extent))])
    return factor_of


def bell_draw(key, dims, deviation, reach, pieces=(), kind=jnp.bfloat16):
    drawn = jax.random.normal(key, dims, jnp.float32) * deviation
    if len(pieces) > 0:
        drawn = block_levels(key, dims, pieces, -0.22, 0.18) * drawn
    return jnp.clip(drawn, min=-reach, max=reach).astype(kind)


def setup_inputs(seed: int = 0) -> dict:
    arg_keys = jax.random.split(jax.random.key(seed), 8)
    queries = draw_queries(jax.random.fold_in(arg_keys[7], 71), 0)
    keys = draw_keys(jax.random.fold_in(arg_keys[7], 71), 0)
    gate = bell_draw(arg_keys[2], (BATCH, SEQ, CHANNELS), 1.0, 6.0, ((0, 4), (1, 32)))
    values = bell_draw(arg_keys[3], (BATCH, SEQ, CHANNELS), 1.0, 6.0, ((0, 4), (1, 32)))
    grad_out = bell_draw(arg_keys[4], (BATCH, SEQ, CHANNELS), 0.5, 3.0, ((0, 4), (1, 32)))
    doc_start = draw_doc_start(jax.random.fold_in(arg_keys[7], 71), 0)
    filter_taps = bell_draw(arg_keys[6], (FILT, CHANNELS), FILT ** -0.5, 0.5, (), jnp.float32)
    return dict(queries=queries, keys=keys, gate=gate, values=values, grad_out=grad_out, doc_start=doc_start, filter_taps=filter_taps)


def causal_filter(signal, filter_taps):
    rim_len = FILT - 1
    padded = jnp.pad(signal, ((rim_len, 0), (0, 0)))

    def add_tap(tap_index, summed):
        window = lax.dynamic_slice_in_dim(padded, rim_len - tap_index, SEQ, 0)
        return summed + filter_taps[tap_index][None, :] * window

    return lax.fori_loop(0, FILT, add_tap, jnp.zeros((SEQ, CHANNELS), jnp.float32))


def to_half(array):
    return lax.optimization_barrier(array.astype(jnp.bfloat16)).astype(jnp.float32)


def sequence_grads(query, keyrow, gate, values, grad_out, doc_start, filter_taps):
    highest = lax.Precision.HIGHEST
    score_scale = HEAD_DIM ** -0.5
    rim_len = FILT - 1
    signal = values.astype(jnp.float32)
    mixed = causal_filter(signal, filter_taps)
    gate_f32 = gate.astype(jnp.float32)
    hyena_out = (gate_f32 * mixed).astype(jnp.bfloat16)
    positions = jnp.arange(SEQ, dtype=jnp.int32)
    allowed = (positions[None, :] <= positions[:, None]) & (positions[None, :] >= doc_start[:, None])

    def split_heads(array):
        return array.reshape(SEQ, HEADS, HEAD_DIM).transpose(1, 0, 2)

    def head_grads(packed):
        query_f32 = packed[0].astype(jnp.float32)
        key_f32 = packed[1].astype(jnp.float32)
        hyena_f32 = packed[2].astype(jnp.float32)
        grad_f32 = packed[3].astype(jnp.float32)
        scores = jnp.dot(query_f32, key_f32.T, precision=highest, preferred_element_type=jnp.float32) * score_scale
        masked = jnp.where(allowed, scores, -jnp.inf)
        row_top = jnp.max(masked, -1, keepdims=True)
        weights = jnp.where(allowed, jnp.exp(masked - row_top), 0.0)
        probs = weights / jnp.sum(weights, -1, keepdims=True)
        probs_half = to_half(probs)
        attended = jnp.dot(probs_half, hyena_f32, precision=highest, preferred_element_type=jnp.float32)
        deltas = jnp.sum(grad_f32 * attended, -1)
        dprob = jnp.dot(grad_f32, hyena_f32.T, precision=highest, preferred_element_type=jnp.float32)
        dscore = to_half(probs * (dprob - deltas[:, None]))
        grad_query = jnp.dot(dscore, key_f32, precision=highest, preferred_element_type=jnp.float32) * score_scale
        grad_key = jnp.dot(dscore.T, query_f32, precision=highest, preferred_element_type=jnp.float32) * score_scale
        grad_hyena = jnp.dot(probs_half.T, grad_f32, precision=highest, preferred_element_type=jnp.float32)
        return grad_query, grad_key, grad_hyena

    head_results = lax.map(head_grads, (split_heads(query), split_heads(keyrow), split_heads(hyena_out), split_heads(grad_out)))

    def join_heads(array):
        return array.transpose(1, 0, 2).reshape(SEQ, CHANNELS)

    grad_query = join_heads(head_results[0])
    grad_key = join_heads(head_results[1])
    grad_hyena = join_heads(head_results[2])
    grad_gate = (grad_hyena * mixed).astype(jnp.bfloat16)
    grad_mixed = (grad_hyena * gate_f32).astype(jnp.bfloat16).astype(jnp.float32)
    grad_padded = jnp.pad(grad_mixed, ((0, rim_len), (0, 0)))

    def add_back(tap_index, summed):
        window = lax.dynamic_slice_in_dim(grad_padded, tap_index, SEQ, 0)
        return summed + filter_taps[tap_index][None, :] * window

    grad_values = lax.fori_loop(0, FILT, add_back, jnp.zeros((SEQ, CHANNELS), jnp.float32))
    value_padded = jnp.pad(signal, ((rim_len, 0), (0, 0)))

    def tap_sum(tap_index):
        window = lax.dynamic_slice_in_dim(value_padded, rim_len - tap_index, SEQ, 0)
        return jnp.sum(grad_mixed * window, 0)

    grad_filter = lax.map(tap_sum, jnp.arange(FILT, dtype=jnp.int32))
    return (grad_query.astype(jnp.bfloat16), grad_key.astype(jnp.bfloat16),
            grad_gate, grad_values.astype(jnp.bfloat16), grad_filter)


def reference(queries, keys, gate, values, grad_out, doc_start, filter_taps):
    def one_sequence(packed):
        return sequence_grads(packed[0], packed[1], packed[2], packed[3], packed[4], packed[5], filter_taps)

    results = lax.map(one_sequence, (queries, keys, gate, values, grad_out, doc_start))
    return results[0], results[1], results[2], results[3], jnp.sum(results[4], 0)
```

```python
import functools

import jax
import jax.numpy as jnp
from jax import lax
from jax.experimental import pallas as pl
from jax.experimental.pallas import tpu as pltpu
from jax.sharding import PartitionSpec as P


HEADS = 32
LANES = 128
PAD = 5
QT = 2
WINDOWS = (3, 5, 7)
LOG2E = 1.4426950408889634
F32 = jnp.float32
BF16 = jnp.bfloat16


def contract(a, b, da, db):
    return lax.dot_general(a, b, (((da,), (db,)), ((), ())), preferred_element_type=F32)


def pack_values(values, doc_start):
    blocks = HEADS
    step = 4

    def body(v_ref, d_ref, o_ref):
        doc = jnp.broadcast_to(d_ref[...], (16, LANES))
        row = lax.broadcasted_iota(jnp.int32, (16, LANES), 0)
        high = lax.shift_right_logical(doc, 8)
        low = jnp.bitwise_and(doc, 255)
        info = jnp.where(row == 0, high, jnp.where(row == 1, low, 0)).astype(F32).astype(BF16)
        for h in range(step):
            o_ref[h, 0:LANES] = v_ref[:, h * LANES : (h + 1) * LANES]
            o_ref[h, LANES : LANES + 16] = info

    return pl.pallas_call(
        body,
        grid=(blocks // step,),
        in_specs=[
            pl.BlockSpec((LANES, step * LANES), lambda i: (0, i)),
            pl.BlockSpec((1, LANES), lambda i: (0, 0)),
        ],
        out_specs=pl.BlockSpec((step, LANES + 16, LANES), lambda i: (i, 0, 0)),
        out_shape=jax.ShapeDtypeStruct((blocks, LANES + 16, LANES), BF16),
        cost_estimate=pl.CostEstimate(flops=0, bytes_accessed=2 << 20, transcendentals=0),
        name="pack_values",
    )(values, doc_start)


def pack_many(*arrays):
    count = len(arrays)
    step = 4

    def body(*refs):
        o_ref = refs[-1]
        for a in range(count):
            for h in range(step):
                o_ref[h, a] = refs[a][:, h * LANES : (h + 1) * LANES]

    return pl.pallas_call(
        body,
        grid=(HEADS // step,),
        in_specs=[pl.BlockSpec((LANES, step * LANES), lambda i: (0, i))] * count,
        out_specs=pl.BlockSpec((step, count, LANES, LANES), lambda i: (i, 0, 0, 0)),
        out_shape=jax.ShapeDtypeStruct((HEADS, count, LANES, LANES), BF16),
        cost_estimate=pl.CostEstimate(flops=0, bytes_accessed=count << 21, transcendentals=0),
        name="pack_many",
    )(*arrays)


def unpack_many(packed, count, types):
    step = 4

    def body(*refs):
        for a in range(count):
            for h in range(step):
                refs[1 + a][:, h * LANES : (h + 1) * LANES] = refs[0][h, a].astype(types[a])

    return pl.pallas_call(
        body,
        grid=(HEADS // step,),
        in_specs=[pl.BlockSpec((step, count, LANES, LANES), lambda i: (i, 0, 0, 0))],
        out_specs=[pl.BlockSpec((LANES, step * LANES), lambda i: (0, i))] * count,
        out_shape=[jax.ShapeDtypeStruct((LANES, HEADS * LANES), t) for t in types],
        cost_estimate=pl.CostEstimate(flops=0, bytes_accessed=count << 21, transcendentals=0),
        name="unpack_many",
    )(packed)


def toeplitz(wt, c):
    w = wt[pl.ds(c, 1), :]
    z = jnp.concatenate([w, jnp.zeros((1, LANES), F32)], 1)
    rows = pltpu.roll(jnp.broadcast_to(z, (LANES, 2 * LANES)), 0, 1, stride=1, stride_axis=0)
    high = rows.astype(BF16)
    low = (rows - high.astype(F32)).astype(BF16)
    return high, low


SLOT = 40


def conv_forward(me, recv, filter_taps):
    blocks = recv.shape[0]

    def body(me_ref, v_ref, taps_ref, mixed_ref, xt, yt, wt):
        wt[...] = taps_ref[...].T

        def clear(c, carry):
            xt[pl.ds(c * SLOT, 8), :] = jnp.zeros((8, LANES), F32)
            return carry

        lax.fori_loop(0, LANES, clear, 0, unroll=8)
        for b in range(blocks):
            xt[pl.ds(8 + b, LANES, stride=SLOT), :] = v_ref[b].astype(F32).T

        def channel(c, carry):
            high, low = toeplitz(wt, c)
            rhs = jnp.concatenate(
                [
                    jnp.concatenate([high[:, :LANES], low[:, :LANES]], 1),
                    jnp.concatenate([high[:, LANES:], low[:, LANES:]], 1),
                ],
                0,
            )
            now = xt[pl.ds(c * SLOT + 8, blocks), :]
            back = xt[pl.ds(c * SLOT + 7, blocks), :]
            lhs = jnp.concatenate([now, back], 1).astype(BF16)
            y = jnp.dot(lhs, rhs, preferred_element_type=F32)
            yt[pl.ds(c * blocks, blocks), :] = y[:, :LANES] + y[:, LANES:]
            return carry

        lax.fori_loop(0, LANES, channel, 0, unroll=4)
        for b in range(blocks):
            mixed_ref[b] = yt[pl.ds(b, LANES, stride=blocks), :].T

    return pl.pallas_call(
        body,
        grid_spec=pltpu.PrefetchScalarGridSpec(
            num_scalar_prefetch=1,
            grid=(1,),
            in_specs=[
                pl.BlockSpec((blocks, LANES, LANES), lambda i, m: (0, 0, 0)),
                pl.BlockSpec((LANES, LANES), lambda i, m: (0, m[0])),
            ],
            out_specs=pl.BlockSpec((blocks, LANES, LANES), lambda i, m: (0, 0, 0)),
            scratch_shapes=[
                pltpu.VMEM((LANES * SLOT, LANES), F32),
                pltpu.VMEM((LANES * blocks, LANES), F32),
                pltpu.VMEM((LANES, LANES), F32),
            ],
        ),
        out_shape=jax.ShapeDtypeStruct((blocks, LANES, LANES), F32),
        cost_estimate=pl.CostEstimate(
            flops=2 * LANES * blocks * 256 * 256 * 4, bytes_accessed=4 << 20, transcendentals=0
        ),
        name="conv_forward",
    )(me, recv, filter_taps)


def attention(need, packed, recv, mixed):
    blocks = packed.shape[0]
    rows = (blocks + PAD) * LANES
    scale = LANES ** (-0.5)
    factor = scale * LOG2E
    width = QT * LANES
    tiles = blocks // QT

    def body(need_ref, q_ref, k_ref, g_ref, d_ref, info_ref, mixed_ref, out_ref, gm_ref, ks, hs, kt, dk, dv, st):
        pad = PAD * LANES
        ks[0:pad, :] = jnp.zeros((pad, LANES), BF16)
        hs[0:pad, :] = jnp.zeros((pad, LANES), BF16)
        kt[:, 0:pad] = jnp.zeros((LANES, pad), BF16)
        dk[...] = jnp.zeros_like(dk)
        dv[...] = jnp.zeros_like(dv)
        for b in range(blocks):
            at = pad + b * LANES
            key = k_ref[b]
            ks[at : at + LANES, :] = key
            kt[:, at : at + LANES] = key.T
            hs[at : at + LANES, :] = (g_ref[b].astype(F32) * mixed_ref[b]).astype(BF16)
            info = info_ref[b].astype(F32)
            st[b // QT, 0:1, (b % QT) * LANES : (b % QT + 1) * LANES] = info[0:1] * 256.0 + info[1:2]

        def tile(i, window):
            span = window * LANES
            first = pl.multiple_of((QT * i + QT - window) * LANES + pad, LANES)
            q = q_ref[pl.ds(QT * i, QT)].reshape(width, LANES)
            d = d_ref[pl.ds(QT * i, QT)].reshape(width, LANES)
            start = st[i, 0:1, :].astype(jnp.int32) - (first - pad)
            s = contract(ks[pl.ds(first, span), :], q, 1, 1)
            kpos = lax.broadcasted_iota(jnp.int32, (span, width), 0)
            qpos = lax.broadcasted_iota(jnp.int32, (span, width), 1) + (window - QT) * LANES
            allowed = (kpos >= start) & (kpos <= qpos)
            s = jnp.where(allowed, s, -1e30)
            top = jnp.max(s, 0, keepdims=True) * factor
            p = jnp.exp2(s * factor - top)
            p = p * (1.0 / jnp.sum(p, 0, keepdims=True))
            half = p.astype(BF16)
            dp = contract(hs[pl.ds(first, span), :], d, 1, 1)
            delta = jnp.sum(half.astype(F32) * dp, 0, keepdims=True)
            ds = (p * (dp - delta)).astype(BF16)
            dv[pl.ds(first, span), :] += jnp.dot(half, d, preferred_element_type=F32)
            dk[pl.ds(first, span), :] += jnp.dot(ds, q, preferred_element_type=F32)
            dq = jnp.dot(kt[:, pl.ds(first, span)], ds, preferred_element_type=F32) * scale
            for j in range(QT):
                out_ref[QT * i + j, 0] = dq[:, j * LANES : (j + 1) * LANES].T.astype(BF16)

        def step(i, carry):
            count = need_ref[i]
            low = 0
            for window in WINDOWS:
                pl.when((count > low) & (count <= window))(functools.partial(tile, i, window))
                low = window
            return carry

        lax.fori_loop(0, tiles, step, 0)
        for b in range(blocks):
            at = pad + b * LANES
            out_ref[b, 1] = (dk[at : at + LANES, :] * scale).astype(BF16)
            gh = dv[at : at + LANES, :]
            out_ref[b, 2] = (gh * mixed_ref[b]).astype(BF16)
            gm_ref[b] = (gh * g_ref[b].astype(F32)).astype(BF16)

    def piece(a):
        return pl.BlockSpec((blocks, None, LANES, LANES), lambda i, n: (0, a, 0, 0))

    whole = pl.BlockSpec((blocks, LANES, LANES), lambda i, n: (0, 0, 0))
    return pl.pallas_call(
        body,
        grid_spec=pltpu.PrefetchScalarGridSpec(
            num_scalar_prefetch=1,
            grid=(1,),
            in_specs=[piece(0), piece(1), piece(2), piece(3),
                      pl.BlockSpec((blocks, 16, LANES), lambda i, n: (0, 8, 0)), whole],
            out_specs=[pl.BlockSpec((blocks, 3, LANES, LANES), lambda i, n: (0, 0, 0, 0)), whole],
            scratch_shapes=[
                pltpu.VMEM((rows, LANES), BF16),
                pltpu.VMEM((rows, LANES), BF16),
                pltpu.VMEM((LANES, rows), BF16),
                pltpu.VMEM((rows, LANES), F32),
                pltpu.VMEM((rows, LANES), F32),
                pltpu.VMEM((tiles, 8, width), F32),
            ],
        ),
        out_shape=[
            jax.ShapeDtypeStruct((blocks, 3, LANES, LANES), BF16),
            jax.ShapeDtypeStruct((blocks, LANES, LANES), BF16),
        ],
        cost_estimate=pl.CostEstimate(
            flops=10 * 896 * 4096 * 128, bytes_accessed=10 << 20, transcendentals=896 * 4096
        ),
        name="attention",
    )(need, packed, packed, packed, packed, recv, mixed)


def conv_backward(me, grad_mixed, recv, filter_taps):
    blocks = recv.shape[0]

    def body(me_ref, gm_ref, v_ref, taps_ref, out_ref, gf_ref, xt, gt, yt, wt, at):
        wt[...] = taps_ref[...].T

        def clear(c, carry):
            xt[pl.ds(c * SLOT, 8), :] = jnp.zeros((8, LANES), F32)
            gt[pl.ds(c * SLOT + blocks, 8), :] = jnp.zeros((8, LANES), F32)
            return carry

        lax.fori_loop(0, LANES, clear, 0, unroll=8)
        for b in range(blocks):
            xt[pl.ds(8 + b, LANES, stride=SLOT), :] = v_ref[b].astype(F32).T
            gt[pl.ds(b, LANES, stride=SLOT), :] = gm_ref[b].astype(F32).T
        t_at = lax.broadcasted_iota(jnp.int32, (LANES, LANES), 0)
        s_at = lax.broadcasted_iota(jnp.int32, (LANES, LANES), 1)
        lower = s_at <= t_at

        def channel(c, carry):
            high, low = toeplitz(wt, c)
            rhs = jnp.concatenate([high, low], 0)
            now = gt[pl.ds(c * SLOT, blocks), :].astype(BF16)
            after = gt[pl.ds(c * SLOT + 1, blocks), :].astype(BF16)
            y = contract(jnp.concatenate([now, after], 1), rhs, 1, 1)
            yt[pl.ds(c * blocks, blocks), :] = y[:, :LANES] + y[:, LANES:]
            value = xt[pl.ds(c * SLOT + 8, blocks), :]
            back = xt[pl.ds(c * SLOT + 7, blocks), :]
            m = contract(now, jnp.concatenate([value, back], 1).astype(BF16), 0, 0)
            d = jnp.where(lower, m[:, :LANES], m[:, LANES:])
            total = d[0:8]
            for j in range(1, LANES // 8):
                total = total + pltpu.roll(d[8 * j : 8 * j + 8], LANES - 8 * j, 1)
            at[pl.ds(c * 8, 8), :] = total
            return carry

        lax.fori_loop(0, LANES, channel, 0, unroll=4)
        for b in range(blocks):
            out_ref[b, 0] = yt[pl.ds(b, LANES, stride=blocks), :].T.astype(BF16)
        total = at[pl.ds(0, LANES, stride=8), :]
        for r in range(1, 8):
            total = total + pltpu.roll(at[pl.ds(r, LANES, stride=8), :], LANES - r, 1)
        flip = jnp.where(s_at == jnp.bitwise_and(LANES - t_at, LANES - 1), 1.0, 0.0).astype(F32)
        gf_ref[...] = lax.dot_general(
            flip, total, (((1,), (1,)), ((), ())), precision=lax.Precision.HIGHEST,
            preferred_element_type=F32,
        )

    return pl.pallas_call(
        body,
        grid_spec=pltpu.PrefetchScalarGridSpec(
            num_scalar_prefetch=1,
            grid=(1,),
            in_specs=[
                pl.BlockSpec((blocks, LANES, LANES), lambda i, m: (0, 0, 0)),
                pl.BlockSpec((blocks, LANES, LANES), lambda i, m: (0, 0, 0)),
                pl.BlockSpec((LANES, LANES), lambda i, m: (0, m[0])),
            ],
            out_specs=[
                pl.BlockSpec((blocks, 1, LANES, LANES), lambda i, m: (0, 0, 0, 0)),
                pl.BlockSpec((LANES, LANES), lambda i, m: (0, 0)),
            ],
            scratch_shapes=[
                pltpu.VMEM((LANES * SLOT, LANES), F32),
                pltpu.VMEM((LANES * SLOT, LANES), F32),
                pltpu.VMEM((LANES * blocks, LANES), F32),
                pltpu.VMEM((LANES, LANES), F32),
                pltpu.VMEM((LANES * 8, LANES), F32),
            ],
        ),
        out_shape=[
            jax.ShapeDtypeStruct((blocks, 2, LANES, LANES), BF16),
            jax.ShapeDtypeStruct((LANES, LANES), F32),
        ],
        cost_estimate=pl.CostEstimate(
            flops=2 * LANES * blocks * 256 * 256 * 4, bytes_accessed=4 << 20, transcendentals=0
        ),
        name="conv_backward",
    )(me, grad_mixed, recv, filter_taps)


def exchange(packed):
    return lax.all_to_all(packed, "ctx", 0, 0, tiled=True)


def on_device(queries, keys, gate, values, grad_out, doc_start, filter_taps):
    me = lax.axis_index("ctx").astype(jnp.int32)[None]
    recv = exchange(pack_values(values[0], doc_start))
    packed = exchange(pack_many(queries[0], keys[0], gate[0], grad_out[0]))
    mixed = conv_forward(me, recv, filter_taps)
    blocks = recv.shape[0]
    info = recv[:, LANES : LANES + 2, 0].astype(jnp.int32)
    starts = info[:, 0] * 256 + info[:, 1]
    first = starts[::QT]
    need = QT * jnp.arange(1, blocks // QT + 1, dtype=jnp.int32) - first // LANES
    grads, grad_mixed = attention(need, packed, recv, mixed)
    grads = exchange(grads)
    last, grad_taps = conv_backward(me, grad_mixed, recv, filter_taps)
    grad_taps = grad_taps + lax.ppermute(grad_taps, "dp", [(0, 1), (1, 0), (2, 3), (3, 2)])
    grad_taps = grad_taps + lax.ppermute(grad_taps, "dp", [(0, 2), (2, 0), (1, 3), (3, 1)])
    last = last.at[:, 1].set(jnp.broadcast_to(grad_taps.astype(BF16)[None], (blocks, LANES, LANES)))
    last = exchange(last)
    grad_query, grad_key, grad_gate = unpack_many(grads, 3, (BF16, BF16, BF16))
    grad_values, grad_filter = unpack_many(last, 2, (BF16, F32))
    return grad_query[None], grad_key[None], grad_gate[None], grad_values[None], grad_filter


def solution(mesh):
    placed = P("dp", "ctx", None)
    return jax.shard_map(
        on_device,
        mesh=mesh,
        in_specs=(placed, placed, placed, placed, placed, P("dp", "ctx"), P()),
        out_specs=(placed, placed, placed, placed, P()),
        check_vma=False,
    )
```

```python
import functools

import jax
import jax.numpy as jnp
from jax import lax
from jax.experimental import pallas as pl
from jax.experimental.pallas import tpu as pltpu
from jax.sharding import PartitionSpec as P


HEADS = 32
LANES = 128
PAD = 5
QT = 2
TWIN = 2
WINDOWS = (2, 3, 4, 5, 6, 7)
LOG2E = 1.4426950408889634
F32 = jnp.float32
BF16 = jnp.bfloat16


def contract(a, b, da, db):
    return lax.dot_general(a, b, (((da,), (db,)), ((), ())), preferred_element_type=F32)


def pack(arrays, doc_start=None):
    count = len(arrays)
    step = HEADS // 2
    extra = 0 if doc_start is None else INFO

    def body(*refs):
        o_ref = refs[-1]
        for a in range(count):
            for h in range(step):
                o_ref[h, a * LANES : (a + 1) * LANES] = refs[a][:, h * LANES : (h + 1) * LANES]
        if extra:
            doc = jnp.broadcast_to(refs[count][...], (INFO, LANES))
            row = lax.broadcasted_iota(jnp.int32, (INFO, LANES), 0)
            high = lax.shift_right_logical(doc, 8)
            low = jnp.bitwise_and(doc, 255)
            info = jnp.where(row == 0, high, jnp.where(row == 1, low, 0)).astype(F32).astype(BF16)
            for h in range(step):
                o_ref[h, count * LANES : count * LANES + INFO] = info

    rows = count * LANES + extra
    specs = [pl.BlockSpec((LANES, step * LANES), lambda i: (0, i))] * count
    if extra:
        arrays = arrays + (doc_start,)
        specs = specs + [pl.BlockSpec((1, LANES), lambda i: (0, 0))]
    return pl.pallas_call(
        body,
        grid=(HEADS // step,),
        in_specs=specs,
        out_specs=pl.BlockSpec((step, rows, LANES), lambda i: (i, 0, 0)),
        out_shape=jax.ShapeDtypeStruct((HEADS, rows, LANES), BF16),
        cost_estimate=pl.CostEstimate(flops=0, bytes_accessed=count << 21, transcendentals=0),
        name="pack",
    )(*arrays)


def unpack(packed, types):
    count = len(types)
    step = HEADS // 2

    def body(*refs):
        for a in range(count):
            for h in range(step):
                piece = refs[0][h, a * LANES : (a + 1) * LANES]
                refs[1 + a][:, h * LANES : (h + 1) * LANES] = piece.astype(types[a])

    return pl.pallas_call(
        body,
        grid=(HEADS // step,),
        in_specs=[pl.BlockSpec((step, count * LANES, LANES), lambda i: (i, 0, 0))],
        out_specs=[pl.BlockSpec((LANES, step * LANES), lambda i: (0, i))] * count,
        out_shape=[jax.ShapeDtypeStruct((LANES, HEADS * LANES), t) for t in types],
        cost_estimate=pl.CostEstimate(flops=0, bytes_accessed=count << 21, transcendentals=0),
        compiler_params=pltpu.CompilerParams(vmem_limit_bytes=SMALL),
        name="unpack",
    )(packed)


def toeplitz(wt, c):
    w = wt[pl.ds(c, 1), :]
    z = jnp.concatenate([w, jnp.zeros((1, LANES), F32)], 1)
    rows = pltpu.roll(jnp.broadcast_to(z, (LANES, 2 * LANES)), 0, 1, stride=1, stride_axis=0)
    high = rows.astype(BF16)
    low = (rows - high.astype(F32)).astype(BF16)
    return high, low


SLOT = 40
INFO = 8
SMALL = 24 << 20


def conv_forward(me, recv, filter_taps):
    blocks = recv.shape[0]

    def body(me_ref, v_ref, taps_ref, mixed_ref, xt, yt, wt):
        wt[...] = taps_ref[...].T

        def clear(c, carry):
            xt[pl.ds(c * SLOT, 8), :] = jnp.zeros((8, LANES), F32)
            return carry

        lax.fori_loop(0, LANES, clear, 0, unroll=8)
        for b in range(blocks):
            xt[pl.ds(8 + b, LANES, stride=SLOT), :] = v_ref[b].T.astype(F32)

        def channel(c, carry):
            high, low = toeplitz(wt, c)
            rhs = jnp.concatenate(
                [
                    jnp.concatenate([high[:, :LANES], low[:, :LANES]], 1),
                    jnp.concatenate([high[:, LANES:], low[:, LANES:]], 1),
                ],
                0,
            )
            now = xt[pl.ds(c * SLOT + 8, blocks), :]
            back = xt[pl.ds(c * SLOT + 7, blocks), :]
            lhs = jnp.concatenate([now, back], 1).astype(BF16)
            y = jnp.dot(lhs, rhs, preferred_element_type=F32)
            yt[pl.ds(c * blocks, blocks), :] = y[:, :LANES] + y[:, LANES:]
            return carry

        lax.fori_loop(0, LANES, channel, 0, unroll=4)
        for b in range(blocks):
            mixed_ref[b] = yt[pl.ds(b, LANES, stride=blocks), :].T

    return pl.pallas_call(
        body,
        grid_spec=pltpu.PrefetchScalarGridSpec(
            num_scalar_prefetch=1,
            grid=(1,),
            in_specs=[
                pl.BlockSpec((blocks, LANES, LANES), lambda i, m: (0, 0, 0)),
                pl.BlockSpec((LANES, LANES), lambda i, m: (0, m[0])),
            ],
            out_specs=pl.BlockSpec((blocks, LANES, LANES), lambda i, m: (0, 0, 0)),
            scratch_shapes=[
                pltpu.VMEM((LANES * SLOT, LANES), F32),
                pltpu.VMEM((LANES * blocks, LANES), F32),
                pltpu.VMEM((LANES, LANES), F32),
            ],
        ),
        out_shape=jax.ShapeDtypeStruct((blocks, LANES, LANES), F32),
        cost_estimate=pl.CostEstimate(
            flops=2 * LANES * blocks * 256 * 256 * 4, bytes_accessed=4 << 20, transcendentals=0
        ),
        name="conv_forward",
    )(me, recv, filter_taps)


CHUNK = 8
FLUSH = TWIN * QT


def attention(need, packed, recv, mixed):
    blocks = packed.shape[0]
    rows = (blocks + PAD) * LANES
    scale = LANES ** (-0.5)
    factor = scale * LOG2E
    width = QT * LANES
    tiles = blocks // QT
    chunks = blocks // CHUNK
    steps = tiles // TWIN
    pad = PAD * LANES

    def body(need_ref, packed_ref, info_ref, mixed_hbm, out_hbm, gm_hbm,
             q_ref, k_ref, g_ref, d_ref, mixed_ref, out_ref, gm_ref, ks, hs, kt, dk, dv, st, in_sem, out_sem):
        def arrivals(c):
            at = pl.ds(c * CHUNK, CHUNK)
            moves = []
            for a, ref in enumerate((q_ref, k_ref, g_ref, d_ref)):
                source = packed_ref.at[at, pl.ds(a * LANES, LANES)]
                moves.append(pltpu.make_async_copy(source, ref.at[at], in_sem.at[c, a]))
            moves.append(pltpu.make_async_copy(mixed_hbm.at[at], mixed_ref.at[at], in_sem.at[c, 4]))
            return moves

        def departures(f):
            at = pl.ds(f * FLUSH, FLUSH)
            return [
                pltpu.make_async_copy(out_ref.at[at], out_hbm.at[at], out_sem.at[f, 0]),
                pltpu.make_async_copy(gm_ref.at[at], gm_hbm.at[at], out_sem.at[f, 1]),
            ]

        for c in range(chunks):
            for move in arrivals(c):
                move.start()
        ks[0:pad, :] = jnp.zeros((pad, LANES), BF16)
        hs[0:pad, :] = jnp.zeros((pad, LANES), BF16)
        kt[:, 0:pad] = jnp.zeros((LANES, pad), BF16)
        dk[...] = jnp.zeros_like(dk)
        dv[...] = jnp.zeros_like(dv)
        for b in range(blocks):
            info = info_ref[b].astype(F32)
            st[b // QT, 0:1, (b % QT) * LANES : (b % QT + 1) * LANES] = info[0:1] * 256.0 + info[1:2]

        def prepare(c):
            for move in arrivals(c):
                move.wait()
            for u in range(CHUNK):
                b = c * CHUNK + u
                at = pl.multiple_of(pad + b * LANES, LANES)
                key = k_ref[b]
                ks[pl.ds(at, LANES), :] = key
                kt[:, pl.ds(at, LANES)] = key.T
                hs[pl.ds(at, LANES), :] = (g_ref[b].astype(F32) * mixed_ref[b]).astype(BF16)

        def finish(f):
            for u in range(FLUSH):
                b = f * FLUSH + u
                at = pl.multiple_of(pad + b * LANES, LANES)
                out_ref[b, LANES : 2 * LANES] = (dk[pl.ds(at, LANES), :] * scale).astype(BF16)
                gh = dv[pl.ds(at, LANES), :]
                out_ref[b, 2 * LANES : 3 * LANES] = (gh * mixed_ref[b]).astype(BF16)
                gm_ref[b] = (gh * g_ref[b].astype(F32)).astype(BF16)
            for move in departures(f):
                move.start()

        def tiles_of(g, window):
            span = window * LANES
            kpos = lax.broadcasted_iota(jnp.int32, (span, width), 0)
            qpos = lax.broadcasted_iota(jnp.int32, (span, width), 1) + (window - QT) * LANES
            held = []
            for u in range(TWIN):
                i = TWIN * g + u
                first = pl.multiple_of((QT * i + QT - window) * LANES + pad, LANES)
                q = q_ref[pl.ds(QT * i, QT)].reshape(width, LANES)
                d = d_ref[pl.ds(QT * i, QT)].reshape(width, LANES)
                start = st[i, 0:1, :].astype(jnp.int32) - (first - pad)
                s = contract(ks[pl.ds(first, span), :], q, 1, 1)
                s = jnp.where((kpos >= start) & (kpos <= qpos), s, -1e30)
                top = jnp.max(s, 0, keepdims=True) * factor
                p = jnp.exp2(s * factor - top)
                p = p * (1.0 / jnp.sum(p, 0, keepdims=True))
                half = p.astype(BF16)
                dp = contract(hs[pl.ds(first, span), :], d, 1, 1)
                delta = jnp.sum(half.astype(F32) * dp, 0, keepdims=True)
                ds = (p * (dp - delta)).astype(BF16)
                held.append((i, first, q, d, half, ds))
            for i, first, q, d, half, ds in held:
                dq = jnp.dot(kt[:, pl.ds(first, span)], ds, preferred_element_type=F32) * scale
                for j in range(QT):
                    out_ref[QT * i + j, 0:LANES] = dq[:, j * LANES : (j + 1) * LANES].T.astype(BF16)
            for i, first, q, d, half, ds in held:
                dv[pl.ds(first, span), :] += jnp.dot(half, d, preferred_element_type=F32)
                dk[pl.ds(first, span), :] += jnp.dot(ds, q, preferred_element_type=F32)

        def step(g, carry):
            pl.when(g % (CHUNK // FLUSH) == 0)(lambda: prepare(g // (CHUNK // FLUSH)))
            count = need_ref[TWIN * g]
            for u in range(1, TWIN):
                count = jnp.maximum(count, need_ref[TWIN * g + u])
            low = 0
            for window in WINDOWS:
                pl.when((count > low) & (count <= window))(functools.partial(tiles_of, g, window))
                low = window
            pl.when(g >= 2)(lambda: finish(g - 2))
            return carry

        lax.fori_loop(0, steps, step, 0)
        for f in range(steps - 2, steps):
            finish(f)
        for f in range(steps):
            for move in departures(f):
                move.wait()

    anywhere = pl.BlockSpec(memory_space=pl.ANY)
    piece = pltpu.VMEM((blocks, LANES, LANES), BF16)
    return pl.pallas_call(
        body,
        grid_spec=pltpu.PrefetchScalarGridSpec(
            num_scalar_prefetch=1,
            grid=(1,),
            in_specs=[anywhere, pl.BlockSpec((blocks, INFO, LANES), lambda i, n: (0, LANES // INFO, 0)), anywhere],
            out_specs=[anywhere, anywhere],
            scratch_shapes=[
                piece,
                piece,
                piece,
                piece,
                pltpu.VMEM((blocks, LANES, LANES), F32),
                pltpu.VMEM((blocks, 3 * LANES, LANES), BF16),
                piece,
                pltpu.VMEM((rows, LANES), BF16),
                pltpu.VMEM((rows, LANES), BF16),
                pltpu.VMEM((LANES, rows), BF16),
                pltpu.VMEM((rows, LANES), F32),
                pltpu.VMEM((rows, LANES), F32),
                pltpu.VMEM((tiles, 8, width), F32),
                pltpu.SemaphoreType.DMA((chunks, 5)),
                pltpu.SemaphoreType.DMA((steps, 2)),
            ],
        ),
        out_shape=[
            jax.ShapeDtypeStruct((blocks, 3 * LANES, LANES), BF16),
            jax.ShapeDtypeStruct((blocks, LANES, LANES), BF16),
        ],
        cost_estimate=pl.CostEstimate(
            flops=10 * 896 * 4096 * 128, bytes_accessed=10 << 20, transcendentals=896 * 4096
        ),
        name="attention",
    )(need, packed, recv, mixed)


def conv_backward(me, grad_mixed, recv, filter_taps):
    blocks = recv.shape[0]

    def body(me_ref, gm_ref, v_ref, taps_ref, out_ref, gf_ref, xt, gt, yt, wt, at):
        wt[...] = taps_ref[...].T

        def clear(c, carry):
            xt[pl.ds(c * SLOT, 8), :] = jnp.zeros((8, LANES), F32)
            gt[pl.ds(c * SLOT + blocks, 8), :] = jnp.zeros((8, LANES), F32)
            return carry

        lax.fori_loop(0, LANES, clear, 0, unroll=8)
        for b in range(blocks):
            xt[pl.ds(8 + b, LANES, stride=SLOT), :] = v_ref[b].T.astype(F32)
            gt[pl.ds(b, LANES, stride=SLOT), :] = gm_ref[b].T.astype(F32)
        t_at = lax.broadcasted_iota(jnp.int32, (LANES, LANES), 0)
        s_at = lax.broadcasted_iota(jnp.int32, (LANES, LANES), 1)
        lower = s_at <= t_at

        def channel(c, carry):
            high, low = toeplitz(wt, c)
            rhs = jnp.concatenate([high, low], 0)
            now = gt[pl.ds(c * SLOT, blocks), :].astype(BF16)
            after = gt[pl.ds(c * SLOT + 1, blocks), :].astype(BF16)
            y = contract(jnp.concatenate([now, after], 1), rhs, 1, 1)
            yt[pl.ds(c * blocks, blocks), :] = y[:, :LANES] + y[:, LANES:]
            value = xt[pl.ds(c * SLOT + 8, blocks), :]
            back = xt[pl.ds(c * SLOT + 7, blocks), :]
            m = contract(now, jnp.concatenate([value, back], 1).astype(BF16), 0, 0)
            d = jnp.where(lower, m[:, :LANES], m[:, LANES:])
            total = d[0:8]
            for j in range(1, LANES // 8):
                total = total + pltpu.roll(d[8 * j : 8 * j + 8], LANES - 8 * j, 1)
            at[pl.ds(c * 8, 8), :] = total
            return carry

        lax.fori_loop(0, LANES, channel, 0, unroll=4)
        for b in range(blocks):
            out_ref[b] = yt[pl.ds(b, LANES, stride=blocks), :].T.astype(BF16)
        total = at[pl.ds(0, LANES, stride=8), :]
        for r in range(1, 8):
            total = total + pltpu.roll(at[pl.ds(r, LANES, stride=8), :], LANES - r, 1)
        flip = jnp.where(s_at == jnp.bitwise_and(LANES - t_at, LANES - 1), 1.0, 0.0).astype(F32)
        gf_ref[...] = lax.dot_general(
            flip, total, (((1,), (1,)), ((), ())), precision=lax.Precision.HIGHEST,
            preferred_element_type=F32,
        )

    return pl.pallas_call(
        body,
        grid_spec=pltpu.PrefetchScalarGridSpec(
            num_scalar_prefetch=1,
            grid=(1,),
            in_specs=[
                pl.BlockSpec((blocks, LANES, LANES), lambda i, m: (0, 0, 0)),
                pl.BlockSpec((blocks, LANES, LANES), lambda i, m: (0, 0, 0)),
                pl.BlockSpec((LANES, LANES), lambda i, m: (0, m[0])),
            ],
            out_specs=[
                pl.BlockSpec((blocks, LANES, LANES), lambda i, m: (0, 0, 0)),
                pl.BlockSpec((LANES, LANES), lambda i, m: (0, 0)),
            ],
            scratch_shapes=[
                pltpu.VMEM((LANES * SLOT, LANES), F32),
                pltpu.VMEM((LANES * SLOT, LANES), F32),
                pltpu.VMEM((LANES * blocks, LANES), F32),
                pltpu.VMEM((LANES, LANES), F32),
                pltpu.VMEM((LANES * 8, LANES), F32),
            ],
        ),
        out_shape=[
            jax.ShapeDtypeStruct((blocks, 2 * LANES, LANES), BF16),
            jax.ShapeDtypeStruct((LANES, LANES), F32),
        ],
        cost_estimate=pl.CostEstimate(
            flops=2 * LANES * blocks * 256 * 256 * 4, bytes_accessed=4 << 20, transcendentals=0
        ),
        name="conv_backward",
    )(me, grad_mixed, recv, filter_taps)


def exchange(packed):
    return lax.all_to_all(packed, "ctx", 0, 0, tiled=True)


def on_device(queries, keys, gate, values, grad_out, doc_start, filter_taps):
    me = lax.axis_index("ctx").astype(jnp.int32)[None]
    recv = exchange(pack((values[0],), doc_start))
    packed = exchange(pack((queries[0], keys[0], gate[0], grad_out[0])))
    mixed = conv_forward(me, recv, filter_taps)
    blocks = recv.shape[0]
    info = recv[:, LANES : LANES + 2, 0].astype(jnp.int32)
    starts = info[:, 0] * 256 + info[:, 1]
    first = starts[::QT]
    need = QT * jnp.arange(1, blocks // QT + 1, dtype=jnp.int32) - first // LANES
    grads, grad_mixed = attention(need, packed, recv, mixed)
    grads = exchange(grads)
    last, grad_taps = conv_backward(me, grad_mixed, recv, filter_taps)
    grad_taps = grad_taps + lax.ppermute(grad_taps, "dp", [(0, 1), (1, 0), (2, 3), (3, 2)])
    grad_taps = grad_taps + lax.ppermute(grad_taps, "dp", [(0, 2), (2, 0), (1, 3), (3, 1)])
    shared = jnp.broadcast_to(grad_taps.astype(BF16)[None], (blocks, LANES, LANES))
    last = exchange(last.at[:, LANES:].set(shared))
    grad_query, grad_key, grad_gate = unpack(grads, (BF16, BF16, BF16))
    grad_values, grad_filter = unpack(last, (BF16, F32))
    return grad_query[None], grad_key[None], grad_gate[None], grad_values[None], grad_filter


def solution(mesh):
    placed = P("dp", "ctx", None)
    return jax.shard_map(
        on_device,
        mesh=mesh,
        in_specs=(placed, placed, placed, placed, placed, P("dp", "ctx"), P()),
        out_specs=(placed, placed, placed, placed, P()),
        check_vma=False,
    )
```

```python
import functools

import jax
import jax.numpy as jnp
from jax import lax
from jax.experimental import pallas as pl
from jax.experimental.pallas import tpu as pltpu
from jax.sharding import PartitionSpec as P


HEADS = 32
LANES = 128
PAD = 5
QT = 2
TWIN = 2
WINDOWS = (2, 3, 4, 5, 6, 7)
LOG2E = 1.4426950408889634
F32 = jnp.float32
BF16 = jnp.bfloat16


def contract(a, b, da, db):
    return lax.dot_general(a, b, (((da,), (db,)), ((), ())), preferred_element_type=F32)


def pack(arrays, doc_start=None):
    count = len(arrays)
    step = HEADS // 2
    extra = 0 if doc_start is None else INFO

    def body(*refs):
        o_ref = refs[-1]
        for a in range(count):
            for h in range(step):
                o_ref[h, a * LANES : (a + 1) * LANES] = refs[a][:, h * LANES : (h + 1) * LANES]
        if extra:
            doc = jnp.broadcast_to(refs[count][...], (INFO, LANES))
            row = lax.broadcasted_iota(jnp.int32, (INFO, LANES), 0)
            high = lax.shift_right_logical(doc, 8)
            low = jnp.bitwise_and(doc, 255)
            info = jnp.where(row == 0, high, jnp.where(row == 1, low, 0)).astype(F32).astype(BF16)
            for h in range(step):
                o_ref[h, count * LANES : count * LANES + INFO] = info

    rows = count * LANES + extra
    specs = [pl.BlockSpec((LANES, step * LANES), lambda i: (0, i))] * count
    if extra:
        arrays = arrays + (doc_start,)
        specs = specs + [pl.BlockSpec((1, LANES), lambda i: (0, 0))]
    return pl.pallas_call(
        body,
        grid=(HEADS // step,),
        in_specs=specs,
        out_specs=pl.BlockSpec((step, rows, LANES), lambda i: (i, 0, 0)),
        out_shape=jax.ShapeDtypeStruct((HEADS, rows, LANES), BF16),
        cost_estimate=pl.CostEstimate(flops=0, bytes_accessed=count << 21, transcendentals=0),
        name="pack",
    )(*arrays)


def unpack(packed, types):
    count = len(types)
    step = HEADS // 2

    def body(*refs):
        for a in range(count):
            for h in range(step):
                piece = refs[0][h, a * LANES : (a + 1) * LANES]
                refs[1 + a][:, h * LANES : (h + 1) * LANES] = piece.astype(types[a])

    return pl.pallas_call(
        body,
        grid=(HEADS // step,),
        in_specs=[pl.BlockSpec((step, count * LANES, LANES), lambda i: (i, 0, 0))],
        out_specs=[pl.BlockSpec((LANES, step * LANES), lambda i: (0, i))] * count,
        out_shape=[jax.ShapeDtypeStruct((LANES, HEADS * LANES), t) for t in types],
        cost_estimate=pl.CostEstimate(flops=0, bytes_accessed=count << 21, transcendentals=0),
        compiler_params=pltpu.CompilerParams(vmem_limit_bytes=SMALL),
        name="unpack",
    )(packed)


def toeplitz(wt, c):
    w = wt[pl.ds(c, 1), :]
    z = jnp.concatenate([w, jnp.zeros((1, LANES), F32)], 1)
    rows = pltpu.roll(jnp.broadcast_to(z, (LANES, 2 * LANES)), 0, 1, stride=1, stride_axis=0)
    high = rows.astype(BF16)
    low = (rows - high.astype(F32)).astype(BF16)
    return high, low


SLOT = 40
INFO = 8
HALF = LANES // 2
SMALL = 24 << 20


def conv_forward(me, recv, filter_taps):
    blocks = recv.shape[0]

    def body(me_ref, v_ref, taps_ref, mixed_ref, xt, yt, wt):
        wt[...] = taps_ref[...].T

        def clear(c, carry):
            xt[pl.ds(c * SLOT, 8), :] = jnp.zeros((8, LANES), F32)
            return carry

        lax.fori_loop(0, LANES, clear, 0, unroll=8)
        for b in range(blocks):
            xt[pl.ds(8 + b, LANES, stride=SLOT), :] = v_ref[b].T.astype(F32)

        def channel(c, carry):
            high, low = toeplitz(wt, c)
            rhs = jnp.concatenate(
                [
                    jnp.concatenate([high[:, :LANES], low[:, :LANES]], 1),
                    jnp.concatenate([high[:, LANES:], low[:, LANES:]], 1),
                ],
                0,
            )
            now = xt[pl.ds(c * SLOT + 8, blocks), :]
            back = xt[pl.ds(c * SLOT + 7, blocks), :]
            lhs = jnp.concatenate([now, back], 1).astype(BF16)
            y = jnp.dot(lhs, rhs, preferred_element_type=F32)
            yt[pl.ds(c * blocks, blocks), :] = y[:, :LANES] + y[:, LANES:]
            return carry

        lax.fori_loop(0, LANES, channel, 0, unroll=4)
        for b in range(blocks):
            mixed_ref[b] = yt[pl.ds(b, LANES, stride=blocks), :].T

    return pl.pallas_call(
        body,
        grid_spec=pltpu.PrefetchScalarGridSpec(
            num_scalar_prefetch=1,
            grid=(1,),
            in_specs=[
                pl.BlockSpec((blocks, LANES, LANES), lambda i, m: (0, 0, 0)),
                pl.BlockSpec((LANES, LANES), lambda i, m: (0, m[0])),
            ],
            out_specs=pl.BlockSpec((blocks, LANES, LANES), lambda i, m: (0, 0, 0)),
            scratch_shapes=[
                pltpu.VMEM((LANES * SLOT, LANES), F32),
                pltpu.VMEM((LANES * blocks, LANES), F32),
                pltpu.VMEM((LANES, LANES), F32),
            ],
        ),
        out_shape=jax.ShapeDtypeStruct((blocks, LANES, LANES), F32),
        cost_estimate=pl.CostEstimate(
            flops=2 * LANES * blocks * 256 * 256 * 4, bytes_accessed=4 << 20, transcendentals=0
        ),
        name="conv_forward",
    )(me, recv, filter_taps)


CHUNK = 8
FLUSH = TWIN * QT


def attention(need, packed, recv, mixed):
    blocks = packed.shape[0]
    rows = (blocks + PAD) * LANES
    scale = LANES ** (-0.5)
    factor = scale * LOG2E
    width = QT * LANES
    tiles = blocks // QT
    chunks = blocks // CHUNK
    steps = tiles // TWIN
    pad = PAD * LANES

    def body(need_ref, packed_ref, info_ref, mixed_hbm, out_hbm, gm_hbm,
             q_ref, k_ref, g_ref, d_ref, mixed_ref, out_ref, gm_ref, ks, hs, kt, dk, dv, st, in_sem, out_sem):
        def arrivals(c):
            at = pl.ds(c * CHUNK, CHUNK)
            moves = []
            for a, ref in enumerate((q_ref, k_ref, g_ref, d_ref)):
                source = packed_ref.at[at, pl.ds(a * LANES, LANES)]
                moves.append(pltpu.make_async_copy(source, ref.at[at], in_sem.at[c, a]))
            moves.append(pltpu.make_async_copy(mixed_hbm.at[at], mixed_ref.at[at], in_sem.at[c, 4]))
            return moves

        def departures(f):
            at = pl.ds(f * FLUSH, FLUSH)
            return [
                pltpu.make_async_copy(out_ref.at[at], out_hbm.at[at], out_sem.at[f, 0]),
                pltpu.make_async_copy(gm_ref.at[at], gm_hbm.at[at], out_sem.at[f, 1]),
            ]

        for c in range(chunks):
            for move in arrivals(c):
                move.start()
        ks[0:pad, :] = jnp.zeros((pad, LANES), BF16)
        hs[0:pad, :] = jnp.zeros((pad, LANES), BF16)
        kt[:, 0:pad] = jnp.zeros((LANES, pad), BF16)
        dk[...] = jnp.zeros_like(dk)
        dv[...] = jnp.zeros_like(dv)
        for b in range(blocks):
            info = info_ref[b].astype(F32)
            st[b // QT, 0:1, (b % QT) * LANES : (b % QT + 1) * LANES] = info[0:1] * 256.0 + info[1:2]

        def prepare(c):
            for move in arrivals(c):
                move.wait()
            for u in range(CHUNK):
                b = c * CHUNK + u
                at = pl.multiple_of(pad + b * LANES, LANES)
                key = k_ref[b]
                ks[pl.ds(at, LANES), :] = key
                kt[:, pl.ds(at, LANES)] = key.T
                hs[pl.ds(at, LANES), :] = (g_ref[b].astype(F32) * mixed_ref[b]).astype(BF16)

        def finish(f):
            for u in range(FLUSH):
                b = f * FLUSH + u
                at = pl.multiple_of(pad + b * LANES, LANES)
                out_ref[b, LANES : 2 * LANES] = (dk[pl.ds(at, LANES), :] * scale).astype(BF16)
                gh = dv[pl.ds(at, LANES), :]
                out_ref[b, 2 * LANES : 3 * LANES] = (gh * mixed_ref[b]).astype(BF16)
                gm_ref[b] = (gh * g_ref[b].astype(F32)).astype(BF16)
            for move in departures(f):
                move.start()

        def tiles_of(g, window):
            span = window * LANES
            kpos = lax.broadcasted_iota(jnp.int32, (span, width), 0)
            qpos = lax.broadcasted_iota(jnp.int32, (span, width), 1) + (window - QT) * LANES
            held = []
            for u in range(TWIN):
                i = TWIN * g + u
                first = pl.multiple_of((QT * i + QT - window) * LANES + pad, LANES)
                q = q_ref[pl.ds(QT * i, QT)].reshape(width, LANES)
                d = d_ref[pl.ds(QT * i, QT)].reshape(width, LANES)
                start = st[i, 0:1, :].astype(jnp.int32) - (first - pad)
                s = contract(ks[pl.ds(first, span), :], q, 1, 1)
                s = jnp.where((kpos >= start) & (kpos <= qpos), s, -1e30)
                top = jnp.max(s, 0, keepdims=True) * factor
                p = jnp.exp2(s * factor - top)
                p = p * (1.0 / jnp.sum(p, 0, keepdims=True))
                half = p.astype(BF16)
                dp = contract(hs[pl.ds(first, span), :], d, 1, 1)
                delta = jnp.sum(half.astype(F32) * dp, 0, keepdims=True)
                ds = (p * (dp - delta)).astype(BF16)
                held.append((i, first, q, d, half, ds))
            for i, first, q, d, half, ds in held:
                dq = jnp.dot(kt[:, pl.ds(first, span)], ds, preferred_element_type=F32) * scale
                for j in range(QT):
                    out_ref[QT * i + j, 0:LANES] = dq[:, j * LANES : (j + 1) * LANES].T.astype(BF16)
            for i, first, q, d, half, ds in held:
                dv[pl.ds(first, span), :] += jnp.dot(half, d, preferred_element_type=F32)
                dk[pl.ds(first, span), :] += jnp.dot(ds, q, preferred_element_type=F32)

        def step(g, carry):
            pl.when(g % (CHUNK // FLUSH) == 0)(lambda: prepare(g // (CHUNK // FLUSH)))
            count = need_ref[TWIN * g]
            for u in range(1, TWIN):
                count = jnp.maximum(count, need_ref[TWIN * g + u])
            low = 0
            for window in WINDOWS:
                pl.when((count > low) & (count <= window))(functools.partial(tiles_of, g, window))
                low = window
            pl.when(g >= 2)(lambda: finish(g - 2))
            return carry

        lax.fori_loop(0, steps, step, 0)
        for f in range(steps - 2, steps):
            finish(f)
        for f in range(steps):
            for move in departures(f):
                move.wait()

    anywhere = pl.BlockSpec(memory_space=pl.ANY)
    piece = pltpu.VMEM((blocks, LANES, LANES), BF16)
    return pl.pallas_call(
        body,
        grid_spec=pltpu.PrefetchScalarGridSpec(
            num_scalar_prefetch=1,
            grid=(1,),
            in_specs=[anywhere, pl.BlockSpec((blocks, INFO, LANES), lambda i, n: (0, LANES // INFO, 0)), anywhere],
            out_specs=[anywhere, anywhere],
            scratch_shapes=[
                piece,
                piece,
                piece,
                piece,
                pltpu.VMEM((blocks, LANES, LANES), F32),
                pltpu.VMEM((blocks, 3 * LANES, LANES), BF16),
                piece,
                pltpu.VMEM((rows, LANES), BF16),
                pltpu.VMEM((rows, LANES), BF16),
                pltpu.VMEM((LANES, rows), BF16),
                pltpu.VMEM((rows, LANES), F32),
                pltpu.VMEM((rows, LANES), F32),
                pltpu.VMEM((tiles, 8, width), F32),
                pltpu.SemaphoreType.DMA((chunks, 5)),
                pltpu.SemaphoreType.DMA((steps, 2)),
            ],
        ),
        out_shape=[
            jax.ShapeDtypeStruct((blocks, 3 * LANES, LANES), BF16),
            jax.ShapeDtypeStruct((blocks, LANES, LANES), BF16),
        ],
        cost_estimate=pl.CostEstimate(
            flops=10 * 896 * 4096 * 128, bytes_accessed=10 << 20, transcendentals=896 * 4096
        ),
        name="attention",
    )(need, packed, recv, mixed)


def conv_backward(me, grad_mixed, recv, filter_taps):
    blocks = recv.shape[0]

    def body(me_ref, gm_ref, v_ref, taps_ref, out_ref, gf_ref, xt, gt, yt, wt, at):
        wt[...] = taps_ref[...].T

        def clear(c, carry):
            xt[pl.ds(c * SLOT, 8), :] = jnp.zeros((8, LANES), F32)
            gt[pl.ds(c * SLOT + blocks, 8), :] = jnp.zeros((8, LANES), F32)
            return carry

        lax.fori_loop(0, LANES, clear, 0, unroll=8)
        for b in range(blocks):
            xt[pl.ds(8 + b, LANES, stride=SLOT), :] = v_ref[b].T.astype(F32)
            gt[pl.ds(b, LANES, stride=SLOT), :] = gm_ref[b].T.astype(F32)
        t_at = lax.broadcasted_iota(jnp.int32, (LANES, LANES), 0)
        s_at = lax.broadcasted_iota(jnp.int32, (LANES, LANES), 1)
        lower = s_at <= t_at

        def channel(c, carry):
            high, low = toeplitz(wt, c)
            rhs = jnp.concatenate([high, low], 0)
            now = gt[pl.ds(c * SLOT, blocks), :].astype(BF16)
            after = gt[pl.ds(c * SLOT + 1, blocks), :].astype(BF16)
            y = contract(jnp.concatenate([now, after], 1), rhs, 1, 1)
            yt[pl.ds(c * blocks, blocks), :] = y[:, :LANES] + y[:, LANES:]
            value = xt[pl.ds(c * SLOT + 8, blocks), :]
            back = xt[pl.ds(c * SLOT + 7, blocks), :]
            m = contract(now, jnp.concatenate([value, back], 1).astype(BF16), 0, 0)
            d = jnp.where(lower, m[:, :LANES], m[:, LANES:])
            total = d[0:8]
            for j in range(1, LANES // 8):
                total = total + pltpu.roll(d[8 * j : 8 * j + 8], LANES - 8 * j, 1)
            at[pl.ds(c * 8, 8), :] = total
            return carry

        lax.fori_loop(0, LANES, channel, 0, unroll=4)
        for b in range(blocks):
            out_ref[b] = yt[pl.ds(b, LANES, stride=blocks), :].T.astype(BF16)
        total = at[pl.ds(0, LANES, stride=8), :]
        for r in range(1, 8):
            total = total + pltpu.roll(at[pl.ds(r, LANES, stride=8), :], LANES - r, 1)
        flip = jnp.where(s_at == jnp.bitwise_and(LANES - t_at, LANES - 1), 1.0, 0.0).astype(F32)
        gf_ref[...] = lax.dot_general(
            flip, total, (((1,), (1,)), ((), ())), precision=lax.Precision.HIGHEST,
            preferred_element_type=F32,
        )

    return pl.pallas_call(
        body,
        grid_spec=pltpu.PrefetchScalarGridSpec(
            num_scalar_prefetch=1,
            grid=(1,),
            in_specs=[
                pl.BlockSpec((blocks, LANES, LANES), lambda i, m: (0, 0, 0)),
                pl.BlockSpec((blocks, LANES, LANES), lambda i, m: (0, 0, 0)),
                pl.BlockSpec((LANES, LANES), lambda i, m: (0, m[0])),
            ],
            out_specs=[
                pl.BlockSpec((blocks, LANES, LANES), lambda i, m: (0, 0, 0)),
                pl.BlockSpec((LANES, LANES), lambda i, m: (0, 0)),
            ],
            scratch_shapes=[
                pltpu.VMEM((LANES * SLOT, LANES), F32),
                pltpu.VMEM((LANES * SLOT, LANES), F32),
                pltpu.VMEM((LANES * blocks, LANES), F32),
                pltpu.VMEM((LANES, LANES), F32),
                pltpu.VMEM((LANES * 8, LANES), F32),
            ],
        ),
        out_shape=[
            jax.ShapeDtypeStruct((blocks, LANES + HALF, LANES), BF16),
            jax.ShapeDtypeStruct((LANES, LANES), F32),
        ],
        cost_estimate=pl.CostEstimate(
            flops=2 * LANES * blocks * 256 * 256 * 4, bytes_accessed=4 << 20, transcendentals=0
        ),
        compiler_params=pltpu.CompilerParams(vmem_limit_bytes=63 << 20),
        name="conv_backward",
    )(me, grad_mixed, recv, filter_taps)


def join_taps(core, last, other):
    step = HEADS // 2

    def body(core_ref, mine_ref, other_ref, out_ref):
        at = pl.multiple_of(core_ref[0] * HALF, HALF)
        rest = pl.multiple_of(HALF - at, HALF)
        for h in range(step):
            lanes = slice(h * LANES, (h + 1) * LANES)
            out_ref[pl.ds(at, HALF), lanes] = mine_ref[h].astype(F32)
            out_ref[pl.ds(rest, HALF), lanes] = other_ref[h].astype(F32)

    return pl.pallas_call(
        body,
        grid_spec=pltpu.PrefetchScalarGridSpec(
            num_scalar_prefetch=1,
            grid=(HEADS // step,),
            in_specs=[
                pl.BlockSpec((step, HALF, LANES), lambda i, c: (i, LANES // HALF, 0)),
                pl.BlockSpec((step, HALF, LANES), lambda i, c: (i, 0, 0)),
            ],
            out_specs=pl.BlockSpec((LANES, step * LANES), lambda i, c: (0, i)),
        ),
        out_shape=jax.ShapeDtypeStruct((LANES, HEADS * LANES), F32),
        cost_estimate=pl.CostEstimate(flops=0, bytes_accessed=3 << 20, transcendentals=0),
        compiler_params=pltpu.CompilerParams(vmem_limit_bytes=SMALL),
        name="join_taps",
    )(core, last, other)


def exchange(packed):
    return lax.all_to_all(packed, "ctx", 0, 0, tiled=True)


def on_device(queries, keys, gate, values, grad_out, doc_start, filter_taps):
    me = lax.axis_index("ctx").astype(jnp.int32)[None]
    recv = exchange(pack((values[0],), doc_start))
    packed = exchange(pack((queries[0], keys[0], gate[0], grad_out[0])))
    mixed = conv_forward(me, recv, filter_taps)
    blocks = recv.shape[0]
    info = recv[:, LANES : LANES + 2, 0].astype(jnp.int32)
    starts = info[:, 0] * 256 + info[:, 1]
    first = starts[::QT]
    need = QT * jnp.arange(1, blocks // QT + 1, dtype=jnp.int32) - first // LANES
    grads, grad_mixed = attention(need, packed, recv, mixed)
    grads = exchange(grads)
    last, grad_taps = conv_backward(me, grad_mixed, recv, filter_taps)
    near = [(0, 1), (1, 0), (2, 3), (3, 2)]
    core = lax.rem(lax.axis_index("dp").astype(jnp.int32), 2)
    mine = lax.dynamic_slice_in_dim(grad_taps, core * HALF, HALF, 0)
    theirs = lax.dynamic_slice_in_dim(grad_taps, (1 - core) * HALF, HALF, 0)
    mine = mine + lax.ppermute(theirs, "dp", near)
    mine = mine + lax.ppermute(mine, "dp", [(0, 2), (2, 0), (1, 3), (3, 1)])
    shared = jnp.broadcast_to(mine.astype(BF16)[None], (blocks, HALF, LANES))
    last = exchange(last.at[:, LANES:].set(shared))
    other = lax.ppermute(last[:, LANES:], "dp", near)
    grad_query, grad_key, grad_gate = unpack(grads, (BF16, BF16, BF16))
    (grad_values,) = unpack(last, (BF16,))
    grad_filter = join_taps(core[None], last, other)
    return grad_query[None], grad_key[None], grad_gate[None], grad_values[None], grad_filter


def solution(mesh):
    placed = P("dp", "ctx", None)
    return jax.shard_map(
        on_device,
        mesh=mesh,
        in_specs=(placed, placed, placed, placed, placed, P("dp", "ctx"), P()),
        out_specs=(placed, placed, placed, placed, P()),
        check_vma=False,
    )
```

```python
import functools

import jax
import jax.numpy as jnp
from jax import lax
from jax.experimental import pallas as pl
from jax.experimental.pallas import tpu as pltpu
from jax.sharding import PartitionSpec as P


HEADS = 32
LANES = 128
PAD = 5
QT = 2
TWIN = 2
WINDOWS = (2, 3, 4, 5, 6, 7)
LOG2E = 1.4426950408889634
F32 = jnp.float32
BF16 = jnp.bfloat16


def contract(a, b, da, db):
    return lax.dot_general(a, b, (((da,), (db,)), ((), ())), preferred_element_type=F32)


def pack(arrays, doc_start=None):
    count = len(arrays)
    step = HEADS // 2
    extra = 0 if doc_start is None else INFO

    def body(*refs):
        o_ref = refs[-1]
        for a in range(count):
            for h in range(step):
                o_ref[h, a * LANES : (a + 1) * LANES] = refs[a][:, h * LANES : (h + 1) * LANES]
        if extra:
            doc = jnp.broadcast_to(refs[count][...], (INFO, LANES))
            row = lax.broadcasted_iota(jnp.int32, (INFO, LANES), 0)
            high = lax.shift_right_logical(doc, 8)
            low = jnp.bitwise_and(doc, 255)
            info = jnp.where(row == 0, high, jnp.where(row == 1, low, 0)).astype(F32).astype(BF16)
            for h in range(step):
                o_ref[h, count * LANES : count * LANES + INFO] = info

    rows = count * LANES + extra
    specs = [pl.BlockSpec((LANES, step * LANES), lambda i: (0, i))] * count
    if extra:
        arrays = arrays + (doc_start,)
        specs = specs + [pl.BlockSpec((1, LANES), lambda i: (0, 0))]
    return pl.pallas_call(
        body,
        grid=(HEADS // step,),
        in_specs=specs,
        out_specs=pl.BlockSpec((step, rows, LANES), lambda i: (i, 0, 0)),
        out_shape=jax.ShapeDtypeStruct((HEADS, rows, LANES), BF16),
        cost_estimate=pl.CostEstimate(flops=0, bytes_accessed=count << 21, transcendentals=0),
        name="pack",
    )(*arrays)


def unpack(packed, types):
    count = len(types)
    step = HEADS // 2

    def body(*refs):
        for a in range(count):
            for h in range(step):
                piece = refs[0][h, a * LANES : (a + 1) * LANES]
                refs[1 + a][:, h * LANES : (h + 1) * LANES] = piece.astype(types[a])

    return pl.pallas_call(
        body,
        grid=(HEADS // step,),
        in_specs=[pl.BlockSpec((step, count * LANES, LANES), lambda i: (i, 0, 0))],
        out_specs=[pl.BlockSpec((LANES, step * LANES), lambda i: (0, i))] * count,
        out_shape=[jax.ShapeDtypeStruct((LANES, HEADS * LANES), t) for t in types],
        cost_estimate=pl.CostEstimate(flops=0, bytes_accessed=count << 21, transcendentals=0),
        compiler_params=pltpu.CompilerParams(vmem_limit_bytes=SMALL),
        name="unpack",
    )(packed)


def toeplitz(wt, c):
    w = wt[pl.ds(c, 1), :]
    z = jnp.concatenate([w, jnp.zeros((1, LANES), F32)], 1)
    rows = pltpu.roll(jnp.broadcast_to(z, (LANES, 2 * LANES)), 0, 1, stride=1, stride_axis=0)
    high = rows.astype(BF16)
    low = (rows - high.astype(F32)).astype(BF16)
    return high, low


SLOT = 40
INFO = 8
HALF = LANES // 2
SMALL = 24 << 20


def conv_forward(me, recv, filter_taps):
    blocks = recv.shape[0]

    def body(me_ref, v_ref, taps_ref, mixed_ref, xt, yt, wt):
        wt[...] = taps_ref[...].T

        def clear(c, carry):
            xt[pl.ds(c * SLOT, 8), :] = jnp.zeros((8, LANES), F32)
            return carry

        lax.fori_loop(0, LANES, clear, 0, unroll=8)
        for b in range(blocks):
            xt[pl.ds(8 + b, LANES, stride=SLOT), :] = v_ref[b].T.astype(F32)

        def channel(c, carry):
            high, low = toeplitz(wt, c)
            rhs = jnp.concatenate(
                [
                    jnp.concatenate([high[:, :LANES], low[:, :LANES]], 1),
                    jnp.concatenate([high[:, LANES:], low[:, LANES:]], 1),
                ],
                0,
            )
            now = xt[pl.ds(c * SLOT + 8, blocks), :]
            back = xt[pl.ds(c * SLOT + 7, blocks), :]
            lhs = jnp.concatenate([now, back], 1).astype(BF16)
            y = jnp.dot(lhs, rhs, preferred_element_type=F32)
            yt[pl.ds(c * blocks, blocks), :] = y[:, :LANES] + y[:, LANES:]
            return carry

        lax.fori_loop(0, LANES, channel, 0, unroll=4)
        for b in range(blocks):
            mixed_ref[b] = yt[pl.ds(b, LANES, stride=blocks), :].T

    return pl.pallas_call(
        body,
        grid_spec=pltpu.PrefetchScalarGridSpec(
            num_scalar_prefetch=1,
            grid=(1,),
            in_specs=[
                pl.BlockSpec((blocks, LANES, LANES), lambda i, m: (0, 0, 0)),
                pl.BlockSpec((LANES, LANES), lambda i, m: (0, m[0])),
            ],
            out_specs=pl.BlockSpec((blocks, LANES, LANES), lambda i, m: (0, 0, 0)),
            scratch_shapes=[
                pltpu.VMEM((LANES * SLOT, LANES), F32),
                pltpu.VMEM((LANES * blocks, LANES), F32),
                pltpu.VMEM((LANES, LANES), F32),
            ],
        ),
        out_shape=jax.ShapeDtypeStruct((blocks, LANES, LANES), F32),
        cost_estimate=pl.CostEstimate(
            flops=2 * LANES * blocks * 256 * 256 * 4, bytes_accessed=4 << 20, transcendentals=0
        ),
        name="conv_forward",
    )(me, recv, filter_taps)


CHUNK = 8
AHEAD = 1
EVERY = 1
FLUSH = TWIN * QT


def attention(need, packed, recv, mixed):
    blocks = packed.shape[0]
    rows = (blocks + PAD) * LANES
    scale = LANES ** (-0.5)
    factor = scale * LOG2E
    width = QT * LANES
    tiles = blocks // QT
    chunks = blocks // CHUNK
    steps = tiles // TWIN
    pad = PAD * LANES

    def body(need_ref, packed_ref, info_ref, mixed_hbm, out_hbm, gm_hbm,
             q_ref, k_ref, g_ref, d_ref, mixed_ref, out_ref, gm_ref, ks, hs, kt, dk, dv, st, in_sem, out_sem):
        def arrivals(c):
            at = pl.ds(c * CHUNK, CHUNK)
            moves = []
            for a, ref in enumerate((q_ref, k_ref, g_ref, d_ref)):
                source = packed_ref.at[at, pl.ds(a * LANES, LANES)]
                moves.append(pltpu.make_async_copy(source, ref.at[at], in_sem.at[c, a]))
            moves.append(pltpu.make_async_copy(mixed_hbm.at[at], mixed_ref.at[at], in_sem.at[c, 4]))
            return moves

        def departures(f):
            at = pl.ds(f * FLUSH, FLUSH)
            return [
                pltpu.make_async_copy(out_ref.at[at], out_hbm.at[at], out_sem.at[f, 0]),
                pltpu.make_async_copy(gm_ref.at[at], gm_hbm.at[at], out_sem.at[f, 1]),
            ]

        def request(c):
            for move in arrivals(c):
                move.start()

        for c in range(AHEAD):
            request(c)
        ks[0:pad, :] = jnp.zeros((pad, LANES), BF16)
        hs[0:pad, :] = jnp.zeros((pad, LANES), BF16)
        kt[:, 0:pad] = jnp.zeros((LANES, pad), BF16)
        dk[...] = jnp.zeros_like(dk)
        dv[...] = jnp.zeros_like(dv)
        for b in range(blocks):
            info = info_ref[b].astype(F32)
            st[b // QT, 0:1, (b % QT) * LANES : (b % QT + 1) * LANES] = info[0:1] * 256.0 + info[1:2]

        def prepare(c):
            for move in arrivals(c):
                move.wait()
            pl.when(c + AHEAD < chunks)(lambda: request(c + AHEAD))
            for u in range(CHUNK):
                b = c * CHUNK + u
                at = pl.multiple_of(pad + b * LANES, LANES)
                key = k_ref[b]
                ks[pl.ds(at, LANES), :] = key
                kt[:, pl.ds(at, LANES)] = key.T
                hs[pl.ds(at, LANES), :] = (g_ref[b].astype(F32) * mixed_ref[b]).astype(BF16)

        def finish(f):
            for u in range(FLUSH):
                b = f * FLUSH + u
                at = pl.multiple_of(pad + b * LANES, LANES)
                out_ref[b, LANES : 2 * LANES] = (dk[pl.ds(at, LANES), :] * scale).astype(BF16)
                gh = dv[pl.ds(at, LANES), :]
                out_ref[b, 2 * LANES : 3 * LANES] = (gh * mixed_ref[b]).astype(BF16)
                gm_ref[b] = (gh * g_ref[b].astype(F32)).astype(BF16)
            for move in departures(f):
                move.start()

        def head(start, s, dp, window, result):
            below = lax.broadcasted_iota(jnp.int32, (LANES, LANES), 0) <= lax.broadcasted_iota(
                jnp.int32, (LANES, LANES), 1
            )
            kpos = lax.broadcasted_iota(jnp.int32, (LANES, LANES), 0)
            halves, grads = [], []
            for j in range(QT):
                count = window - (QT - 1 - j)
                lanes = slice(j * LANES, (j + 1) * LANES)
                scores, weights, probs, half, replies = [], [], [], [], []
                top = None
                for b in range(count):
                    score = jnp.where(
                        kpos >= start[:, lanes] - b * LANES, s[b * LANES : (b + 1) * LANES, lanes], -1e30
                    )
                    if b == count - 1:
                        score = jnp.where(below, score, -1e30)
                    scores.append(score)
                    most = jnp.max(score, 0, keepdims=True)
                    top = most if top is None else jnp.maximum(top, most)
                    yield
                top = top * factor
                total = 0.0
                for b in range(count):
                    weights.append(jnp.exp2(scores[b] * factor - top))
                    total = total + jnp.sum(weights[b], 0, keepdims=True)
                    yield
                share = 1.0 / total
                delta = 0.0
                for b in range(count):
                    probs.append(weights[b] * share)
                    half.append(probs[b].astype(BF16))
                    replies.append(dp[b * LANES : (b + 1) * LANES, lanes])
                    delta = delta + jnp.sum(half[b].astype(F32) * replies[b], 0, keepdims=True)
                    yield
                grad = []
                for b in range(count):
                    grad.append((probs[b] * (replies[b] - delta)).astype(BF16))
                    yield
                gap = [jnp.zeros((LANES, LANES), BF16)] * (window - count)
                halves.append(jnp.concatenate(half + gap, 0))
                grads.append(jnp.concatenate(grad + gap, 0))
            result.append(jnp.concatenate(halves, 1))
            result.append(jnp.concatenate(grads, 1))

        def tail(i, first, q, d, window, result):
            half, ds = result
            span = window * LANES
            dq = jnp.dot(kt[:, pl.ds(first, span)], ds, preferred_element_type=F32) * scale
            for j in range(QT):
                out_ref[QT * i + j, 0:LANES] = dq[:, j * LANES : (j + 1) * LANES].T.astype(BF16)
            yield
            for acc, left, right in ((dv, half, d), (dk, ds, q)):
                acc[pl.ds(first, span), :] += jnp.dot(left, right, preferred_element_type=F32)
                yield

        def tiles_of(g, window):
            span = window * LANES
            before = iter(())
            for u in range(TWIN):
                i = TWIN * g + u
                first = pl.multiple_of((QT * i + QT - window) * LANES + pad, LANES)
                q = q_ref[pl.ds(QT * i, QT)].reshape(width, LANES)
                d = d_ref[pl.ds(QT * i, QT)].reshape(width, LANES)
                start = st[i, 0:1, :].astype(jnp.int32) - (first - pad)
                s = contract(ks[pl.ds(first, span), :], q, 1, 1)
                dp = contract(hs[pl.ds(first, span), :], d, 1, 1)
                result = []
                for at, _ in enumerate(head(start, s, dp, window, result)):
                    if at % (EVERY * window) == 0:
                        next(before, None)
                for _ in before:
                    pass
                before = tail(i, first, q, d, window, result)
            for _ in before:
                pass

        def step(g, carry):
            pl.when(g % (CHUNK // FLUSH) == 0)(lambda: prepare(g // (CHUNK // FLUSH)))
            count = need_ref[TWIN * g]
            for u in range(1, TWIN):
                count = jnp.maximum(count, need_ref[TWIN * g + u])
            low = 0
            for window in WINDOWS:
                pl.when((count > low) & (count <= window))(functools.partial(tiles_of, g, window))
                low = window
            pl.when(g >= 2)(lambda: finish(g - 2))
            return carry

        lax.fori_loop(0, steps, step, 0)
        for f in range(steps - 2, steps):
            finish(f)
        for f in range(steps):
            for move in departures(f):
                move.wait()

    anywhere = pl.BlockSpec(memory_space=pl.ANY)
    piece = pltpu.VMEM((blocks, LANES, LANES), BF16)
    return pl.pallas_call(
        body,
        grid_spec=pltpu.PrefetchScalarGridSpec(
            num_scalar_prefetch=1,
            grid=(1,),
            in_specs=[anywhere, pl.BlockSpec((blocks, INFO, LANES), lambda i, n: (0, LANES // INFO, 0)), anywhere],
            out_specs=[anywhere, anywhere],
            scratch_shapes=[
                piece,
                piece,
                piece,
                piece,
                pltpu.VMEM((blocks, LANES, LANES), F32),
                pltpu.VMEM((blocks, 3 * LANES, LANES), BF16),
                piece,
                pltpu.VMEM((rows, LANES), BF16),
                pltpu.VMEM((rows, LANES), BF16),
                pltpu.VMEM((LANES, rows), BF16),
                pltpu.VMEM((rows, LANES), F32),
                pltpu.VMEM((rows, LANES), F32),
                pltpu.VMEM((tiles, 8, width), F32),
                pltpu.SemaphoreType.DMA((chunks, 5)),
                pltpu.SemaphoreType.DMA((steps, 2)),
            ],
        ),
        out_shape=[
            jax.ShapeDtypeStruct((blocks, 3 * LANES, LANES), BF16),
            jax.ShapeDtypeStruct((blocks, LANES, LANES), BF16),
        ],
        cost_estimate=pl.CostEstimate(
            flops=10 * 896 * 4096 * 128, bytes_accessed=10 << 20, transcendentals=896 * 4096
        ),
        name="attention",
    )(need, packed, recv, mixed)


def conv_backward(me, grad_mixed, recv, filter_taps):
    blocks = recv.shape[0]

    def body(me_ref, gm_ref, v_ref, taps_ref, out_ref, gf_ref, xt, gt, yt, wt, at):
        wt[...] = taps_ref[...].T

        def clear(c, carry):
            xt[pl.ds(c * SLOT, 8), :] = jnp.zeros((8, LANES), F32)
            gt[pl.ds(c * SLOT + blocks, 8), :] = jnp.zeros((8, LANES), F32)
            return carry

        lax.fori_loop(0, LANES, clear, 0, unroll=8)
        for b in range(blocks):
            xt[pl.ds(8 + b, LANES, stride=SLOT), :] = v_ref[b].T.astype(F32)
            gt[pl.ds(b, LANES, stride=SLOT), :] = gm_ref[b].T.astype(F32)
        t_at = lax.broadcasted_iota(jnp.int32, (LANES, LANES), 0)
        s_at = lax.broadcasted_iota(jnp.int32, (LANES, LANES), 1)
        lower = s_at <= t_at

        def channel(c, carry):
            high, low = toeplitz(wt, c)
            rhs = jnp.concatenate([high, low], 0)
            now = gt[pl.ds(c * SLOT, blocks), :].astype(BF16)
            after = gt[pl.ds(c * SLOT + 1, blocks), :].astype(BF16)
            y = contract(jnp.concatenate([now, after], 1), rhs, 1, 1)
            yt[pl.ds(c * blocks, blocks), :] = y[:, :LANES] + y[:, LANES:]
            value = xt[pl.ds(c * SLOT + 8, blocks), :]
            back = xt[pl.ds(c * SLOT + 7, blocks), :]
            m = contract(now, jnp.concatenate([value, back], 1).astype(BF16), 0, 0)
            d = jnp.where(lower, m[:, :LANES], m[:, LANES:])
            total = d[0:8]
            for j in range(1, LANES // 8):
                total = total + pltpu.roll(d[8 * j : 8 * j + 8], LANES - 8 * j, 1)
            at[pl.ds(c * 8, 8), :] = total
            return carry

        lax.fori_loop(0, LANES, channel, 0, unroll=4)
        for b in range(blocks):
            out_ref[b] = yt[pl.ds(b, LANES, stride=blocks), :].T.astype(BF16)
        total = at[pl.ds(0, LANES, stride=8), :]
        for r in range(1, 8):
            total = total + pltpu.roll(at[pl.ds(r, LANES, stride=8), :], LANES - r, 1)
        flip = jnp.where(s_at == jnp.bitwise_and(LANES - t_at, LANES - 1), 1.0, 0.0).astype(F32)
        gf_ref[...] = lax.dot_general(
            flip, total, (((1,), (1,)), ((), ())), precision=lax.Precision.HIGHEST,
            preferred_element_type=F32,
        )

    return pl.pallas_call(
        body,
        grid_spec=pltpu.PrefetchScalarGridSpec(
            num_scalar_prefetch=1,
            grid=(1,),
            in_specs=[
                pl.BlockSpec((blocks, LANES, LANES), lambda i, m: (0, 0, 0)),
                pl.BlockSpec((blocks, LANES, LANES), lambda i, m: (0, 0, 0)),
                pl.BlockSpec((LANES, LANES), lambda i, m: (0, m[0])),
            ],
            out_specs=[
                pl.BlockSpec((blocks, LANES, LANES), lambda i, m: (0, 0, 0)),
                pl.BlockSpec((LANES, LANES), lambda i, m: (0, 0)),
            ],
            scratch_shapes=[
                pltpu.VMEM((LANES * SLOT, LANES), F32),
                pltpu.VMEM((LANES * SLOT, LANES), F32),
                pltpu.VMEM((LANES * blocks, LANES), F32),
                pltpu.VMEM((LANES, LANES), F32),
                pltpu.VMEM((LANES * 8, LANES), F32),
            ],
        ),
        out_shape=[
            jax.ShapeDtypeStruct((blocks, LANES + HALF, LANES), BF16),
            jax.ShapeDtypeStruct((LANES, LANES), F32),
        ],
        cost_estimate=pl.CostEstimate(
            flops=2 * LANES * blocks * 256 * 256 * 4, bytes_accessed=4 << 20, transcendentals=0
        ),
        compiler_params=pltpu.CompilerParams(vmem_limit_bytes=63 << 20),
        name="conv_backward",
    )(me, grad_mixed, recv, filter_taps)


def join_taps(core, last, other):
    step = HEADS // 2

    def body(core_ref, mine_ref, other_ref, out_ref):
        at = pl.multiple_of(core_ref[0] * HALF, HALF)
        rest = pl.multiple_of(HALF - at, HALF)
        for h in range(step):
            lanes = slice(h * LANES, (h + 1) * LANES)
            out_ref[pl.ds(at, HALF), lanes] = mine_ref[h].astype(F32)
            out_ref[pl.ds(rest, HALF), lanes] = other_ref[h].astype(F32)

    return pl.pallas_call(
        body,
        grid_spec=pltpu.PrefetchScalarGridSpec(
            num_scalar_prefetch=1,
            grid=(HEADS // step,),
            in_specs=[
                pl.BlockSpec((step, HALF, LANES), lambda i, c: (i, LANES // HALF, 0)),
                pl.BlockSpec((step, HALF, LANES), lambda i, c: (i, 0, 0)),
            ],
            out_specs=pl.BlockSpec((LANES, step * LANES), lambda i, c: (0, i)),
        ),
        out_shape=jax.ShapeDtypeStruct((LANES, HEADS * LANES), F32),
        cost_estimate=pl.CostEstimate(flops=0, bytes_accessed=3 << 20, transcendentals=0),
        compiler_params=pltpu.CompilerParams(vmem_limit_bytes=SMALL),
        name="join_taps",
    )(core, last, other)


def exchange(packed):
    return lax.all_to_all(packed, "ctx", 0, 0, tiled=True)


def on_device(queries, keys, gate, values, grad_out, doc_start, filter_taps):
    me = lax.axis_index("ctx").astype(jnp.int32)[None]
    recv = exchange(pack((values[0],), doc_start))
    packed = exchange(pack((queries[0], keys[0], gate[0], grad_out[0])))
    mixed = conv_forward(me, recv, filter_taps)
    blocks = recv.shape[0]
    info = recv[:, LANES : LANES + 2, 0].astype(jnp.int32)
    starts = info[:, 0] * 256 + info[:, 1]
    first = starts[::QT]
    need = QT * jnp.arange(1, blocks // QT + 1, dtype=jnp.int32) - first // LANES
    grads, grad_mixed = attention(need, packed, recv, mixed)
    grads = exchange(grads)
    last, grad_taps = conv_backward(me, grad_mixed, recv, filter_taps)
    near = [(0, 1), (1, 0), (2, 3), (3, 2)]
    core = lax.rem(lax.axis_index("dp").astype(jnp.int32), 2)
    mine = lax.dynamic_slice_in_dim(grad_taps, core * HALF, HALF, 0)
    theirs = lax.dynamic_slice_in_dim(grad_taps, (1 - core) * HALF, HALF, 0)
    mine = mine + lax.ppermute(theirs, "dp", near)
    mine = mine + lax.ppermute(mine, "dp", [(0, 2), (2, 0), (1, 3), (3, 1)])
    shared = jnp.broadcast_to(mine.astype(BF16)[None], (blocks, HALF, LANES))
    last = exchange(last.at[:, LANES:].set(shared))
    other = lax.ppermute(last[:, LANES:], "dp", near)
    grad_query, grad_key, grad_gate = unpack(grads, (BF16, BF16, BF16))
    (grad_values,) = unpack(last, (BF16,))
    grad_filter = join_taps(core[None], last, other)
    return grad_query[None], grad_key[None], grad_gate[None], grad_values[None], grad_filter


def solution(mesh):
    placed = P("dp", "ctx", None)
    return jax.shard_map(
        on_device,
        mesh=mesh,
        in_specs=(placed, placed, placed, placed, placed, P("dp", "ctx"), P()),
        out_specs=(placed, placed, placed, placed, P()),
        check_vma=False,
    )
```

```python
import functools

import jax
import jax.numpy as jnp
from jax import lax
from jax.experimental import pallas as pl
from jax.experimental.pallas import tpu as pltpu
from jax.sharding import PartitionSpec as P


HEADS = 32
LANES = 128
PAD = 5
QT = 2
TWIN = 2
WINDOWS = (2, 3, 4, 5, 6, 7)
LOG2E = 1.4426950408889634
F32 = jnp.float32
BF16 = jnp.bfloat16


def contract(a, b, da, db):
    return lax.dot_general(a, b, (((da,), (db,)), ((), ())), preferred_element_type=F32)


def pack(arrays, doc_start=None):
    count = len(arrays)
    step = HEADS // 2
    extra = 0 if doc_start is None else INFO

    def body(*refs):
        o_ref = refs[-1]
        for a in range(count):
            for h in range(step):
                o_ref[h, a * LANES : (a + 1) * LANES] = refs[a][:, h * LANES : (h + 1) * LANES]
        if extra:
            doc = jnp.broadcast_to(refs[count][...], (INFO, LANES))
            row = lax.broadcasted_iota(jnp.int32, (INFO, LANES), 0)
            high = lax.shift_right_logical(doc, 8)
            low = jnp.bitwise_and(doc, 255)
            info = jnp.where(row == 0, high, jnp.where(row == 1, low, 0)).astype(F32).astype(BF16)
            for h in range(step):
                o_ref[h, count * LANES : count * LANES + INFO] = info

    rows = count * LANES + extra
    specs = [pl.BlockSpec((LANES, step * LANES), lambda i: (0, i))] * count
    if extra:
        arrays = arrays + (doc_start,)
        specs = specs + [pl.BlockSpec((1, LANES), lambda i: (0, 0))]
    return pl.pallas_call(
        body,
        grid=(HEADS // step,),
        in_specs=specs,
        out_specs=pl.BlockSpec((step, rows, LANES), lambda i: (i, 0, 0)),
        out_shape=jax.ShapeDtypeStruct((HEADS, rows, LANES), BF16),
        cost_estimate=pl.CostEstimate(flops=0, bytes_accessed=count << 21, transcendentals=0),
        name="pack",
    )(*arrays)


def unpack(packed, types):
    count = len(types)
    step = HEADS // 2

    def body(*refs):
        for a in range(count):
            for h in range(step):
                piece = refs[0][h, a * LANES : (a + 1) * LANES]
                refs[1 + a][:, h * LANES : (h + 1) * LANES] = piece.astype(types[a])

    return pl.pallas_call(
        body,
        grid=(HEADS // step,),
        in_specs=[pl.BlockSpec((step, count * LANES, LANES), lambda i: (i, 0, 0))],
        out_specs=[pl.BlockSpec((LANES, step * LANES), lambda i: (0, i))] * count,
        out_shape=[jax.ShapeDtypeStruct((LANES, HEADS * LANES), t) for t in types],
        cost_estimate=pl.CostEstimate(flops=0, bytes_accessed=count << 21, transcendentals=0),
        compiler_params=pltpu.CompilerParams(vmem_limit_bytes=SMALL),
        name="unpack",
    )(packed)


def toeplitz(wt, c):
    w = wt[pl.ds(c, 1), :]
    z = jnp.concatenate([w, jnp.zeros((1, LANES), F32)], 1)
    rows = pltpu.roll(jnp.broadcast_to(z, (LANES, 2 * LANES)), 0, 1, stride=1, stride_axis=0)
    high = rows.astype(BF16)
    low = (rows - high.astype(F32)).astype(BF16)
    return high, low


SLOT = 40
INFO = 8
HALF = LANES // 2
SMALL = 24 << 20


def conv_forward(me, recv, filter_taps):
    blocks = recv.shape[0]

    def body(me_ref, v_ref, taps_ref, mixed_ref, xt, yt, wt):
        wt[...] = taps_ref[...].T

        def clear(c, carry):
            xt[pl.ds(c * SLOT, 8), :] = jnp.zeros((8, LANES), F32)
            return carry

        lax.fori_loop(0, LANES, clear, 0, unroll=8)
        for b in range(blocks):
            xt[pl.ds(8 + b, LANES, stride=SLOT), :] = v_ref[b].T.astype(F32)

        def channel(c, carry):
            high, low = toeplitz(wt, c)
            rhs = jnp.concatenate(
                [
                    jnp.concatenate([high[:, :LANES], low[:, :LANES]], 1),
                    jnp.concatenate([high[:, LANES:], low[:, LANES:]], 1),
                ],
                0,
            )
            now = xt[pl.ds(c * SLOT + 8, blocks), :]
            back = xt[pl.ds(c * SLOT + 7, blocks), :]
            lhs = jnp.concatenate([now, back], 1).astype(BF16)
            y = jnp.dot(lhs, rhs, preferred_element_type=F32)
            yt[pl.ds(c * blocks, blocks), :] = y[:, :LANES] + y[:, LANES:]
            return carry

        lax.fori_loop(0, LANES, channel, 0, unroll=4)
        for b in range(blocks):
            mixed_ref[b] = yt[pl.ds(b, LANES, stride=blocks), :].T

    return pl.pallas_call(
        body,
        grid_spec=pltpu.PrefetchScalarGridSpec(
            num_scalar_prefetch=1,
            grid=(1,),
            in_specs=[
                pl.BlockSpec((blocks, LANES, LANES), lambda i, m: (0, 0, 0)),
                pl.BlockSpec((LANES, LANES), lambda i, m: (0, m[0])),
            ],
            out_specs=pl.BlockSpec((blocks, LANES, LANES), lambda i, m: (0, 0, 0)),
            scratch_shapes=[
                pltpu.VMEM((LANES * SLOT, LANES), F32),
                pltpu.VMEM((LANES * blocks, LANES), F32),
                pltpu.VMEM((LANES, LANES), F32),
            ],
        ),
        out_shape=jax.ShapeDtypeStruct((blocks, LANES, LANES), F32),
        cost_estimate=pl.CostEstimate(
            flops=2 * LANES * blocks * 256 * 256 * 4, bytes_accessed=4 << 20, transcendentals=0
        ),
        name="conv_forward",
    )(me, recv, filter_taps)


CHUNK = 8
AHEAD = 1
EVERY = 1
FLUSH = TWIN * QT


def attention(need, packed, recv, mixed):
    blocks = packed.shape[0]
    rows = (blocks + PAD) * LANES
    scale = LANES ** (-0.5)
    factor = scale * LOG2E
    width = QT * LANES
    tiles = blocks // QT
    chunks = blocks // CHUNK
    steps = tiles // TWIN
    pad = PAD * LANES

    def body(need_ref, packed_ref, info_ref, mixed_hbm, out_hbm, gm_hbm,
             q_ref, k_ref, g_ref, d_ref, mixed_ref, out_ref, gm_ref, ks, hs, kt, dk, dv, st, in_sem, out_sem):
        def arrivals(c):
            at = pl.ds(c * CHUNK, CHUNK)
            moves = []
            for a, ref in enumerate((q_ref, k_ref, g_ref, d_ref)):
                source = packed_ref.at[at, pl.ds(a * LANES, LANES)]
                moves.append(pltpu.make_async_copy(source, ref.at[at], in_sem.at[c, a]))
            moves.append(pltpu.make_async_copy(mixed_hbm.at[at], mixed_ref.at[at], in_sem.at[c, 4]))
            return moves

        def departures(f):
            at = pl.ds(f * FLUSH, FLUSH)
            return [
                pltpu.make_async_copy(out_ref.at[at], out_hbm.at[at], out_sem.at[f, 0]),
                pltpu.make_async_copy(gm_ref.at[at], gm_hbm.at[at], out_sem.at[f, 1]),
            ]

        def request(c):
            for move in arrivals(c):
                move.start()

        for c in range(AHEAD):
            request(c)
        ks[0:pad, :] = jnp.zeros((pad, LANES), BF16)
        hs[0:pad, :] = jnp.zeros((pad, LANES), BF16)
        kt[:, 0:pad] = jnp.zeros((LANES, pad), BF16)
        dk[...] = jnp.zeros_like(dk)
        dv[...] = jnp.zeros_like(dv)
        for b in range(blocks):
            info = info_ref[b].astype(F32)
            st[b // QT, 0:1, (b % QT) * LANES : (b % QT + 1) * LANES] = info[0:1] * 256.0 + info[1:2]

        def prepare(c):
            for move in arrivals(c):
                move.wait()
            pl.when(c + AHEAD < chunks)(lambda: request(c + AHEAD))
            for u in range(CHUNK):
                b = c * CHUNK + u
                at = pl.multiple_of(pad + b * LANES, LANES)
                key = k_ref[b]
                ks[pl.ds(at, LANES), :] = key
                kt[:, pl.ds(at, LANES)] = key.T
                hs[pl.ds(at, LANES), :] = (g_ref[b].astype(F32) * mixed_ref[b]).astype(BF16)

        def finish(f):
            for u in range(FLUSH):
                b = f * FLUSH + u
                at = pl.multiple_of(pad + b * LANES, LANES)
                out_ref[b, LANES : 2 * LANES] = (dk[pl.ds(at, LANES), :] * scale).astype(BF16)
                gh = dv[pl.ds(at, LANES), :]
                out_ref[b, 2 * LANES : 3 * LANES] = (gh * mixed_ref[b]).astype(BF16)
                gm_ref[b] = (gh * g_ref[b].astype(F32)).astype(BF16)
            for move in departures(f):
                move.start()

        def head(start, s, dp, window, result):
            below = lax.broadcasted_iota(jnp.int32, (LANES, LANES), 0) <= lax.broadcasted_iota(
                jnp.int32, (LANES, LANES), 1
            )
            kpos = lax.broadcasted_iota(jnp.int32, (LANES, LANES), 0)
            halves, grads = [], []
            for j in range(QT):
                count = window - (QT - 1 - j)
                lanes = slice(j * LANES, (j + 1) * LANES)
                scores, weights, probs, half, replies = [], [], [], [], []
                top = None
                for b in range(count):
                    score = jnp.where(
                        kpos >= start[:, lanes] - b * LANES, s[b * LANES : (b + 1) * LANES, lanes], -1e30
                    )
                    if b == count - 1:
                        score = jnp.where(below, score, -1e30)
                    scores.append(score)
                    most = jnp.max(score, 0, keepdims=True)
                    top = most if top is None else jnp.maximum(top, most)
                    yield
                top = top * factor
                total = 0.0
                for b in range(count):
                    weights.append(jnp.exp2(scores[b] * factor - top))
                    total = total + jnp.sum(weights[b], 0, keepdims=True)
                    yield
                share = 1.0 / total
                delta = 0.0
                for b in range(count):
                    probs.append(weights[b] * share)
                    half.append(probs[b].astype(BF16))
                    replies.append(dp[b * LANES : (b + 1) * LANES, lanes])
                    delta = delta + jnp.sum(half[b].astype(F32) * replies[b], 0, keepdims=True)
                    yield
                grad = []
                for b in range(count):
                    grad.append((probs[b] * (replies[b] - delta)).astype(BF16))
                    yield
                gap = [jnp.zeros((LANES, LANES), BF16)] * (window - count)
                halves.append(jnp.concatenate(half + gap, 0))
                grads.append(jnp.concatenate(grad + gap, 0))
            result.append(jnp.concatenate(halves, 1))
            result.append(jnp.concatenate(grads, 1))

        def tail(i, first, q, d, window, result):
            half, ds = result
            span = window * LANES
            dq = jnp.dot(kt[:, pl.ds(first, span)], ds, preferred_element_type=F32) * scale
            for j in range(QT):
                out_ref[QT * i + j, 0:LANES] = dq[:, j * LANES : (j + 1) * LANES].T.astype(BF16)
            yield
            for acc, left, right in ((dv, half, d), (dk, ds, q)):
                acc[pl.ds(first, span), :] += jnp.dot(left, right, preferred_element_type=F32)
                yield

        def tiles_of(g, window):
            span = window * LANES
            ready = []

            def scores_of(u):
                i = TWIN * g + u
                first = pl.multiple_of((QT * i + QT - window) * LANES + pad, LANES)
                q = q_ref[pl.ds(QT * i, QT)].reshape(width, LANES)
                d = d_ref[pl.ds(QT * i, QT)].reshape(width, LANES)
                s = contract(ks[pl.ds(first, span), :], q, 1, 1)
                yield
                dp = contract(hs[pl.ds(first, span), :], d, 1, 1)
                ready.append((i, first, q, d, s, dp))
                yield

            for _ in scores_of(0):
                pass
            before = scores_of(1)
            for u in range(TWIN):
                i, first, q, d, s, dp = ready[u]
                start = st[i, 0:1, :].astype(jnp.int32) - (first - pad)
                result = []
                for at, _ in enumerate(head(start, s, dp, window, result)):
                    if at % (EVERY * window) == window // 2:
                        next(before, None)
                for _ in before:
                    pass
                before = tail(i, first, q, d, window, result)
            for _ in before:
                pass

        def step(g, carry):
            pl.when(g % (CHUNK // FLUSH) == 0)(lambda: prepare(g // (CHUNK // FLUSH)))
            count = need_ref[TWIN * g]
            for u in range(1, TWIN):
                count = jnp.maximum(count, need_ref[TWIN * g + u])
            low = 0
            for window in WINDOWS:
                pl.when((count > low) & (count <= window))(functools.partial(tiles_of, g, window))
                low = window
            pl.when(g >= 2)(lambda: finish(g - 2))
            return carry

        lax.fori_loop(0, steps, step, 0)
        for f in range(steps - 2, steps):
            finish(f)
        for f in range(steps):
            for move in departures(f):
                move.wait()

    anywhere = pl.BlockSpec(memory_space=pl.ANY)
    piece = pltpu.VMEM((blocks, LANES, LANES), BF16)
    return pl.pallas_call(
        body,
        grid_spec=pltpu.PrefetchScalarGridSpec(
            num_scalar_prefetch=1,
            grid=(1,),
            in_specs=[anywhere, pl.BlockSpec((blocks, INFO, LANES), lambda i, n: (0, LANES // INFO, 0)), anywhere],
            out_specs=[anywhere, anywhere],
            scratch_shapes=[
                piece,
                piece,
                piece,
                piece,
                pltpu.VMEM((blocks, LANES, LANES), F32),
                pltpu.VMEM((blocks, 3 * LANES, LANES), BF16),
                piece,
                pltpu.VMEM((rows, LANES), BF16),
                pltpu.VMEM((rows, LANES), BF16),
                pltpu.VMEM((LANES, rows), BF16),
                pltpu.VMEM((rows, LANES), F32),
                pltpu.VMEM((rows, LANES), F32),
                pltpu.VMEM((tiles, 8, width), F32),
                pltpu.SemaphoreType.DMA((chunks, 5)),
                pltpu.SemaphoreType.DMA((steps, 2)),
            ],
        ),
        out_shape=[
            jax.ShapeDtypeStruct((blocks, 3 * LANES, LANES), BF16),
            jax.ShapeDtypeStruct((blocks, LANES, LANES), BF16),
        ],
        cost_estimate=pl.CostEstimate(
            flops=10 * 896 * 4096 * 128, bytes_accessed=10 << 20, transcendentals=896 * 4096
        ),
        name="attention",
    )(need, packed, recv, mixed)


def conv_backward(me, grad_mixed, recv, filter_taps):
    blocks = recv.shape[0]

    def body(me_ref, gm_ref, v_ref, taps_ref, out_ref, gf_ref, xt, gt, yt, wt, at):
        wt[...] = taps_ref[...].T

        def clear(c, carry):
            xt[pl.ds(c * SLOT, 8), :] = jnp.zeros((8, LANES), F32)
            gt[pl.ds(c * SLOT + blocks, 8), :] = jnp.zeros((8, LANES), F32)
            return carry

        lax.fori_loop(0, LANES, clear, 0, unroll=8)
        for b in range(blocks):
            xt[pl.ds(8 + b, LANES, stride=SLOT), :] = v_ref[b].T.astype(F32)
            gt[pl.ds(b, LANES, stride=SLOT), :] = gm_ref[b].T.astype(F32)
        t_at = lax.broadcasted_iota(jnp.int32, (LANES, LANES), 0)
        s_at = lax.broadcasted_iota(jnp.int32, (LANES, LANES), 1)
        lower = s_at <= t_at

        def channel(c, carry):
            high, low = toeplitz(wt, c)
            rhs = jnp.concatenate([high, low], 0)
            now = gt[pl.ds(c * SLOT, blocks), :].astype(BF16)
            after = gt[pl.ds(c * SLOT + 1, blocks), :].astype(BF16)
            y = contract(jnp.concatenate([now, after], 1), rhs, 1, 1)
            yt[pl.ds(c * blocks, blocks), :] = y[:, :LANES] + y[:, LANES:]
            value = xt[pl.ds(c * SLOT + 8, blocks), :]
            back = xt[pl.ds(c * SLOT + 7, blocks), :]
            m = contract(now, jnp.concatenate([value, back], 1).astype(BF16), 0, 0)
            d = jnp.where(lower, m[:, :LANES], m[:, LANES:])
            total = d[0:8]
            for j in range(1, LANES // 8):
                total = total + pltpu.roll(d[8 * j : 8 * j + 8], LANES - 8 * j, 1)
            at[pl.ds(c * 8, 8), :] = total
            return carry

        lax.fori_loop(0, LANES, channel, 0, unroll=4)
        for b in range(blocks):
            out_ref[b] = yt[pl.ds(b, LANES, stride=blocks), :].T.astype(BF16)
        total = at[pl.ds(0, LANES, stride=8), :]
        for r in range(1, 8):
            total = total + pltpu.roll(at[pl.ds(r, LANES, stride=8), :], LANES - r, 1)
        flip = jnp.where(s_at == jnp.bitwise_and(LANES - t_at, LANES - 1), 1.0, 0.0).astype(F32)
        gf_ref[...] = lax.dot_general(
            flip, total, (((1,), (1,)), ((), ())), precision=lax.Precision.HIGHEST,
            preferred_element_type=F32,
        )

    return pl.pallas_call(
        body,
        grid_spec=pltpu.PrefetchScalarGridSpec(
            num_scalar_prefetch=1,
            grid=(1,),
            in_specs=[
                pl.BlockSpec((blocks, LANES, LANES), lambda i, m: (0, 0, 0)),
                pl.BlockSpec((blocks, LANES, LANES), lambda i, m: (0, 0, 0)),
                pl.BlockSpec((LANES, LANES), lambda i, m: (0, m[0])),
            ],
            out_specs=[
                pl.BlockSpec((blocks, LANES, LANES), lambda i, m: (0, 0, 0)),
                pl.BlockSpec((LANES, LANES), lambda i, m: (0, 0)),
            ],
            scratch_shapes=[
                pltpu.VMEM((LANES * SLOT, LANES), F32),
                pltpu.VMEM((LANES * SLOT, LANES), F32),
                pltpu.VMEM((LANES * blocks, LANES), F32),
                pltpu.VMEM((LANES, LANES), F32),
                pltpu.VMEM((LANES * 8, LANES), F32),
            ],
        ),
        out_shape=[
            jax.ShapeDtypeStruct((blocks, LANES + HALF, LANES), BF16),
            jax.ShapeDtypeStruct((LANES, LANES), F32),
        ],
        cost_estimate=pl.CostEstimate(
            flops=2 * LANES * blocks * 256 * 256 * 4, bytes_accessed=4 << 20, transcendentals=0
        ),
        compiler_params=pltpu.CompilerParams(vmem_limit_bytes=63 << 20),
        name="conv_backward",
    )(me, grad_mixed, recv, filter_taps)


def join_taps(core, last, other):
    step = HEADS // 2

    def body(core_ref, mine_ref, other_ref, out_ref):
        at = pl.multiple_of(core_ref[0] * HALF, HALF)
        rest = pl.multiple_of(HALF - at, HALF)
        for h in range(step):
            lanes = slice(h * LANES, (h + 1) * LANES)
            out_ref[pl.ds(at, HALF), lanes] = mine_ref[h].astype(F32)
            out_ref[pl.ds(rest, HALF), lanes] = other_ref[h].astype(F32)

    return pl.pallas_call(
        body,
        grid_spec=pltpu.PrefetchScalarGridSpec(
            num_scalar_prefetch=1,
            grid=(HEADS // step,),
            in_specs=[
                pl.BlockSpec((step, HALF, LANES), lambda i, c: (i, LANES // HALF, 0)),
                pl.BlockSpec((step, HALF, LANES), lambda i, c: (i, 0, 0)),
            ],
            out_specs=pl.BlockSpec((LANES, step * LANES), lambda i, c: (0, i)),
        ),
        out_shape=jax.ShapeDtypeStruct((LANES, HEADS * LANES), F32),
        cost_estimate=pl.CostEstimate(flops=0, bytes_accessed=3 << 20, transcendentals=0),
        compiler_params=pltpu.CompilerParams(vmem_limit_bytes=SMALL),
        name="join_taps",
    )(core, last, other)


def exchange(packed):
    return lax.all_to_all(packed, "ctx", 0, 0, tiled=True)


def on_device(queries, keys, gate, values, grad_out, doc_start, filter_taps):
    me = lax.axis_index("ctx").astype(jnp.int32)[None]
    recv = exchange(pack((values[0],), doc_start))
    packed = exchange(pack((queries[0], keys[0], gate[0], grad_out[0])))
    mixed = conv_forward(me, recv, filter_taps)
    blocks = recv.shape[0]
    info = recv[:, LANES : LANES + 2, 0].astype(jnp.int32)
    starts = info[:, 0] * 256 + info[:, 1]
    first = starts[::QT]
    need = QT * jnp.arange(1, blocks // QT + 1, dtype=jnp.int32) - first // LANES
    grads, grad_mixed = attention(need, packed, recv, mixed)
    grads = exchange(grads)
    last, grad_taps = conv_backward(me, grad_mixed, recv, filter_taps)
    near = [(0, 1), (1, 0), (2, 3), (3, 2)]
    core = lax.rem(lax.axis_index("dp").astype(jnp.int32), 2)
    mine = lax.dynamic_slice_in_dim(grad_taps, core * HALF, HALF, 0)
    theirs = lax.dynamic_slice_in_dim(grad_taps, (1 - core) * HALF, HALF, 0)
    mine = mine + lax.ppermute(theirs, "dp", near)
    mine = mine + lax.ppermute(mine, "dp", [(0, 2), (2, 0), (1, 3), (3, 1)])
    shared = jnp.broadcast_to(mine.astype(BF16)[None], (blocks, HALF, LANES))
    last = exchange(last.at[:, LANES:].set(shared))
    other = lax.ppermute(last[:, LANES:], "dp", near)
    grad_query, grad_key, grad_gate = unpack(grads, (BF16, BF16, BF16))
    (grad_values,) = unpack(last, (BF16,))
    grad_filter = join_taps(core[None], last, other)
    return grad_query[None], grad_key[None], grad_gate[None], grad_values[None], grad_filter


def solution(mesh):
    placed = P("dp", "ctx", None)
    return jax.shard_map(
        on_device,
        mesh=mesh,
        in_specs=(placed, placed, placed, placed, placed, P("dp", "ctx"), P()),
        out_specs=(placed, placed, placed, placed, P()),
        check_vma=False,
    )
```
